128 devices in a mesh: pair: 8 (over z, y_hi), walk: 16 (over x, y_lo, core).
Axes of the slice: x: 4, y: 4 (y_hi: 2, y_lo: 2; y = y_hi * 2 + y_lo), z: 4, core: 2. Of those that a mesh axis runs over, the one named last changes fastest.
Arguments:
- cholesky: bfloat16 [1024, 589824], P('walk', 'pair'), may hold values from -0.0078125 to 0.0078125
- fields: bfloat16 [1024, 128], replicated, may hold values from -6 to 6
- orbitals: bfloat16 [128, 192, 768], P(('pair', 'walk')), may hold values from -0.109375 to 0.109375
- cotangent: bfloat16 [128, 192, 768], P(('pair', 'walk')), may hold values from -6 to 6
Outputs:
- orbital_grad: bfloat16 [128, 192, 768], P(('pair', 'walk'))
- cholesky_grad: bfloat16 [1024, 589824], P('walk', 'pair')
- field_grad: float32 [1024, 128], P('walk', 'pair')
The draws below stay inside these ranges and needn't reach their ends.
All inputs are finite; a program needn't handle non-finite values.
Results may differ from the reference program's by a relative error of at most 0.023.
Values may be sent and summed in bfloat16 or wider, within the bound.
No kernel may reach another device: no remote copies, remote signals or barrier semaphores. Data moves between devices by JAX's collectives and lax.ppermute only.
A program may use at most 128 MiB of HBM per device.

```python
import jax
import jax.numpy as jnp
from jax import lax

ORBITALS = 768
ELECTRONS = 192
VEC_DEV = 64
VECTORS = 1024
WALKERS = 128


def level_of(rng, extent, cuts, least, largest):
    factor_of = 1.0
    for axis_at, blocks in cuts:
        heights = jax.random.uniform(jax.random.fold_in(jax.random.fold_in(rng, 6), axis_at), (blocks,), jnp.float32, least / len(cuts), largest / len(cuts))
        factor_of = factor_of * jnp.repeat(jnp.exp(heights), extent[axis_at] // blocks).reshape((-1,) + (1,) * (len(extent) - 1 - axis_at))
    return factor_of


def bell_draw(key, shape, scale, most, split=(), kind=jnp.bfloat16):
    array = jax.random.normal(key, shape, jnp.float32) * scale
    if len(split) > 0:
        array = level_of(key, shape, split, -0.22, 0.18) * array
    return jnp.clip(array, min=-most, max=most).astype(kind)


def setup_inputs(seed: int = 0) -> dict:
    streams_of = jax.random.split(jax.random.key(seed), 5)
    return {
        "cholesky": bell_draw(streams_of[0], (VECTORS, ORBITALS * ORBITALS), (1.2 / (ORBITALS * VECTORS) ** 0.5), 0.0078125, ((0, 16), (1, 8))),
        "fields": bell_draw(streams_of[1], (VECTORS, WALKERS), 1.0, 6.0),
        "orbitals": bell_draw(streams_of[2], (WALKERS, ELECTRONS, ORBITALS), (3.0 / (ELECTRONS * WALKERS) ** 0.5), 0.109375, ((0, 128),)),
        "cotangent": bell_draw(streams_of[3], (WALKERS, ELECTRONS, ORBITALS), 1.0, 6.0, ((0, 128),)),
    }


def taylor_reverse(potential_row, orbit_rows, cotan_rows):
    width = orbit_rows.shape[1]
    matrix = potential_row.reshape(width, width)
    series = [orbit_rows]
    for degree in range(1, 5):
        product = lax.dot_general(series[-1], matrix, (((1,), (1,)), ((), ())), preferred_element_type=jnp.float32)
        series.append((product / degree).astype(jnp.bfloat16))
    seed_wide = cotan_rows.astype(jnp.float32)
    adjoint = [cotan_rows, cotan_rows, cotan_rows, cotan_rows, cotan_rows]
    for degree in (3, 2, 1):
        product = jnp.dot(adjoint[degree + 1], matrix, preferred_element_type=jnp.float32)
        adjoint[degree] = (seed_wide + product / (degree + 1)).astype(jnp.bfloat16)
    orbit_grad = (seed_wide + jnp.dot(adjoint[1], matrix, preferred_element_type=jnp.float32)).astype(jnp.bfloat16)
    gradient = lax.dot_general(adjoint[1], series[0], (((0,), (0,)), ((), ())), preferred_element_type=jnp.float32)
    for degree in range(2, 5):
        gradient = gradient + lax.dot_general(adjoint[degree], series[degree - 1], (((0,), (0,)), ((), ())), preferred_element_type=jnp.float32) / degree
    return orbit_grad, gradient.astype(jnp.bfloat16).reshape(width * width)


def reference(cholesky, fields, orbitals, cotangent):
    windows = VECTORS // VEC_DEV
    chol_windows = cholesky.reshape(windows, VEC_DEV, ORBITALS * ORBITALS)
    field_windows = fields.reshape(windows, VEC_DEV, WALKERS)

    def add_window(running, pieces):
        chol_piece, field_piece = pieces
        window_part = lax.dot_general(field_piece, chol_piece, (((0,), (0,)), ((), ())), preferred_element_type=jnp.float32)
        rounded = lax.optimization_barrier(window_part.astype(jnp.bfloat16))
        return running + rounded.astype(jnp.float32), None

    running, _ = lax.scan(add_window, jnp.zeros((WALKERS, ORBITALS * ORBITALS), jnp.float32), (chol_windows, field_windows))
    potential = running.astype(jnp.bfloat16)

    def one_walker(inputs):
        return taylor_reverse(inputs[0], inputs[1], inputs[2])

    orbital_grad, potential_grad = lax.map(one_walker, (potential, orbitals, cotangent))

    def grad_window(field_piece):
        return jnp.dot(field_piece, potential_grad, preferred_element_type=jnp.float32).astype(jnp.bfloat16)

    cholesky_grad = lax.map(grad_window, field_windows).reshape(VECTORS, ORBITALS * ORBITALS)
    field_grad = lax.dot_general(cholesky, potential_grad, (((1,), (1,)), ((), ())), preferred_element_type=jnp.float32)
    return orbital_grad, cholesky_grad, field_grad
```

```python
import functools

import jax
import jax.numpy as jnp
from jax import lax
from jax.experimental import pallas as pl
from jax.experimental.pallas import tpu as pltpu
from jax.sharding import PartitionSpec as P


BF16 = jnp.bfloat16
F32 = jnp.float32
ALL = ("pair", "walk")
CHUNKS = 3
BLOCK = 2048
LANES = 128


def moved(to):
    pairs = []
    for z in range(4):
        for yh in range(2):
            for x in range(4):
                for yl in range(2):
                    for c in range(2):
                        z2, yh2, x2, yl2, c2 = to(z, yh, x, yl, c)
                        here = ((z * 2 + yh) * 4 + x) * 4 + yl * 2 + c
                        there = (((z2 % 4) * 2 + yh2 % 2) * 4 + x2 % 4) * 4 + (yl2 % 2) * 2 + c2 % 2
                        pairs.append((here, there))
    return pairs


CORE = moved(lambda z, yh, x, yl, c: (z, yh, x, yl, c + 1))
SIDE = moved(lambda z, yh, x, yl, c: (z, yh, x, yl + 1, c))
UP = moved(lambda z, yh, x, yl, c: (z, yh, x + 1, yl, c))
DOWN = moved(lambda z, yh, x, yl, c: (z, yh, x + 3, yl, c))
OTHERS = [(m, dz) for m in range(2) for dz in range(4)]


def across(m, dz):
    return moved(lambda z, yh, x, yl, c: (z + dz, yh + m, x, yl + m, c))


def send(array, pairs):
    return lax.ppermute(array, ALL, pairs)


def added(*terms):
    total = terms[0].astype(F32)
    for term in terms[1:]:
        total = total + term.astype(F32)
    return total.astype(BF16)


def whole(shape):
    return pl.BlockSpec(shape, lambda *_: (0,) * len(shape))


def partial_kernel(groups, at_ref, weights_ref, own_ref, other_ref, *outs):
    rows = jnp.concatenate([own_ref[...], other_ref[...]], axis=0)
    sums = jnp.dot(weights_ref[...], rows, preferred_element_type=F32).astype(BF16)
    for group, out in zip(groups, outs):
        for place, start in enumerate(group):
            out[place * 16 : place * 16 + 16, :] = sums[start : start + 16]


def partial_sums(at, weights, cholesky, other, chunk, groups):
    rows, width = other.shape
    steps = width // BLOCK
    return pl.pallas_call(
        functools.partial(partial_kernel, groups),
        grid_spec=pltpu.PrefetchScalarGridSpec(
            num_scalar_prefetch=1,
            grid=(steps,),
            in_specs=[
                whole(weights.shape),
                pl.BlockSpec((rows, BLOCK), lambda i, at: (0, at[0] * (CHUNKS * steps) + chunk * steps + i)),
                pl.BlockSpec((rows, BLOCK), lambda i, at: (0, i)),
            ],
            out_specs=[pl.BlockSpec((16 * len(g), BLOCK), lambda i, at: (0, i)) for g in groups],
        ),
        out_shape=[jax.ShapeDtypeStruct((16 * len(g), width), BF16) for g in groups],
        cost_estimate=pl.CostEstimate(flops=2 * 128 * 128 * width, bytes_accessed=512 * width, transcendentals=0),
        name="partial_sums",
    )(at, weights, cholesky, other)


def unpack_kernel(depth, width, n_own, *refs):
    own, (other,) = refs[:n_own], refs[n_own : n_own + 1]
    outs, scratch = refs[n_own + 1 : -1], refs[-1]
    across_lanes = width // LANES
    for half, parts in enumerate((own, (other,))):
        for tile in range(depth * across_lanes):
            lanes = slice(tile * LANES, (tile + 1) * LANES)
            total = parts[0][0:8, lanes].astype(F32)
            for part in parts[1:]:
                total = total + part[0:8, lanes].astype(F32)
            scratch[half, tile * 8 : tile * 8 + 8, :] = total
        for walker in range(8):
            for lane in range(across_lanes):
                tall = [
                    scratch[half, pl.ds((top * across_lanes + lane) * 8 + walker, 8, stride=8 * across_lanes), :]
                    for top in range(0, depth, 8)
                ]
                outs[walker][half, :, lane * LANES : (lane + 1) * LANES] = jnp.concatenate(tall, axis=0).astype(BF16)


def unpack(own, other, width):
    depth = other.shape[1] // width
    return pl.pallas_call(
        functools.partial(unpack_kernel, depth, width, len(own)),
        grid=(1,),
        in_specs=[pl.BlockSpec((8, depth * width), lambda i: (0, 0)) for _ in range(len(own) + 1)],
        out_specs=[whole((2, depth, width)) for _ in OTHERS],
        out_shape=[jax.ShapeDtypeStruct((2, depth, width), BF16) for _ in OTHERS],
        scratch_shapes=[pltpu.VMEM((2, depth * width // LANES * 8, LANES), F32)],
        name="unpack",
    )(*own, other)


def pack_kernel(depth, width, *refs):
    blocks, own, other, scratch = refs[:8], refs[8], refs[9], refs[10]
    across_lanes = width // LANES
    for half, out in enumerate((own, other)):
        for walker in range(8):
            for lane in range(across_lanes):
                tall = blocks[walker][half, :, lane * LANES : (lane + 1) * LANES].astype(F32)
                for top in range(0, depth, 8):
                    rows = pl.ds((top * across_lanes + lane) * 8 + walker, 8, stride=8 * across_lanes)
                    scratch[half, rows, :] = tall[top : top + 8]
        for tile in range(depth * across_lanes):
            out[:, tile * LANES : (tile + 1) * LANES] = scratch[half, tile * 8 : tile * 8 + 8, :].astype(BF16)


def pack(blocks):
    _, depth, width = blocks[0].shape
    return pl.pallas_call(
        functools.partial(pack_kernel, depth, width),
        grid=(1,),
        in_specs=[whole((2, depth, width)) for _ in OTHERS],
        out_specs=[whole((8, depth * width))] * 2,
        out_shape=[jax.ShapeDtypeStruct((8, depth * width), BF16)] * 2,
        scratch_shapes=[pltpu.VMEM((2, depth * width // LANES * 8, LANES), F32)],
        name="pack",
    )(*blocks)


def taylor_kernel(n_blocks, depth, at_ref, orbit_ref, cotan_ref, *refs):
    blocks, orbit_out, outs = refs[:n_blocks], refs[n_blocks], refs[n_blocks + 1 : 2 * n_blocks + 1]
    matrix, grad = refs[2 * n_blocks + 1 :]
    for n, block in enumerate(blocks):
        for half in range(2):
            row = pl.multiple_of(at_ref[2 * n + half], 16)
            matrix[pl.ds(row, depth), :] = block[half]
    orbit, cotan = orbit_ref[0], cotan_ref[0]
    seed = cotan.astype(F32)
    series, adjoint = [orbit], [None, None, None, None, cotan]
    for degree in (1, 2, 3):
        product = lax.dot_general(series[-1], matrix[...], (((1,), (1,)), ((), ())), preferred_element_type=F32)
        series.append((product / degree).astype(BF16))
        down = 4 - degree
        product = jnp.dot(adjoint[down + 1], matrix[...], preferred_element_type=F32)
        adjoint[down] = (seed + product / (down + 1)).astype(BF16)
    orbit_out[0] = (seed + jnp.dot(adjoint[1], matrix[...], preferred_element_type=F32)).astype(BF16)
    width = matrix.shape[0]
    for top in range(0, width, 256):
        total = None
        for degree in range(1, 5):
            term = lax.dot_general(
                adjoint[degree][:, top : top + 256], series[degree - 1], (((0,), (0,)), ((), ())), preferred_element_type=F32
            )
            total = term if total is None else total + term / degree
        grad[top : top + 256, :] = total.astype(BF16)
    for n, out in enumerate(outs):
        for half in range(2):
            row = pl.multiple_of(at_ref[2 * n_blocks + 2 * n + half], 16)
            out[half] = grad[pl.ds(row, depth), :]


def taylor(at, orbitals, cotangent, blocks):
    _, depth, width = blocks[0].shape
    n = len(blocks)
    return pl.pallas_call(
        functools.partial(taylor_kernel, n, depth),
        grid_spec=pltpu.PrefetchScalarGridSpec(
            num_scalar_prefetch=1,
            grid=(1,),
            in_specs=[whole(orbitals.shape), whole(cotangent.shape)] + [whole((2, depth, width))] * n,
            out_specs=[whole(orbitals.shape)] + [whole((2, depth, width))] * n,
            scratch_shapes=[pltpu.VMEM((width, width), BF16), pltpu.VMEM((width, width), BF16)],
        ),
        out_shape=[jax.ShapeDtypeStruct(orbitals.shape, BF16)] + [jax.ShapeDtypeStruct((2, depth, width), BF16)] * n,
        name="taylor",
    )(at, orbitals, cotangent, *blocks)


def finish_kernel(n_parts, has_out, at_ref, weights_ref, own_ref, other_ref, field_ref, *refs):
    parts = refs[:n_parts]
    chol_out, other_out, field_out = refs[n_parts + has_out :]

    @pl.when(pl.program_id(0) == 0)
    def _():
        field_out[...] = field_ref[...]

    grads = jnp.concatenate([part[...] for part in parts], axis=0)
    rows = jnp.concatenate([own_ref[...], other_ref[...]], axis=0)
    field_out[...] += lax.dot_general(rows, grads, (((1,), (1,)), ((), ())), preferred_element_type=F32)
    total = jnp.dot(weights_ref[...], grads, preferred_element_type=F32).astype(BF16)
    half = total.shape[0] // 2
    chol_out[...] = total[:half]
    other_out[...] = total[half:]


def finish(at, weights, cholesky, other, field, parts, chunk, out):
    rows, width = other.shape
    steps = width // BLOCK
    here = pl.BlockSpec((rows, BLOCK), lambda i, at: (0, at[0] * (CHUNKS * steps) + chunk * steps + i))
    in_specs = [whole(weights.shape), here, pl.BlockSpec((rows, BLOCK), lambda i, at: (0, i)), whole(field.shape)]
    in_specs += [pl.BlockSpec((part.shape[0], BLOCK), lambda i, at: (0, i)) for part in parts]
    args = [at, weights, cholesky, other, field, *parts]
    aliases = {}
    if out is not None:
        aliases = {len(args): 0}
        args.append(out)
        in_specs.append(pl.BlockSpec(memory_space=pl.ANY))
    return pl.pallas_call(
        functools.partial(finish_kernel, len(parts), int(out is not None)),
        grid_spec=pltpu.PrefetchScalarGridSpec(
            num_scalar_prefetch=1,
            grid=(steps,),
            in_specs=in_specs,
            out_specs=[here, pl.BlockSpec((rows, BLOCK), lambda i, at: (0, i)), whole(field.shape)],
        ),
        out_shape=[
            jax.ShapeDtypeStruct(cholesky.shape, BF16),
            jax.ShapeDtypeStruct((rows, width), BF16),
            jax.ShapeDtypeStruct(field.shape, F32),
        ],
        input_output_aliases=aliases,
        cost_estimate=pl.CostEstimate(flops=4 * 128 * 128 * width, bytes_accessed=768 * width, transcendentals=0),
        name="finish",
    )(*args)


def place_kernel(at_ref, piece_ref, out_in, out_ref):
    out_ref[...] = piece_ref[...]


def place(at, piece, out, chunk):
    rows, width = piece.shape
    steps = width // BLOCK
    return pl.pallas_call(
        place_kernel,
        grid_spec=pltpu.PrefetchScalarGridSpec(
            num_scalar_prefetch=1,
            grid=(steps,),
            in_specs=[pl.BlockSpec((rows, BLOCK), lambda i, at: (0, i)), pl.BlockSpec(memory_space=pl.ANY)],
            out_specs=pl.BlockSpec((rows, BLOCK), lambda i, at: (0, (1 - at[0]) * (CHUNKS * steps) + chunk * steps + i)),
        ),
        out_shape=jax.ShapeDtypeStruct(out.shape, out.dtype),
        input_output_aliases={2: 0},
        name="place",
    )(at, piece, out)


def reduce_side_last(parts):
    p20, p21, p10, p11, p30, p31, p00, p01 = parts
    up, down = send(p20, UP), send(p21, DOWN)
    up_free, down_free = send(p11, UP), send(p30, DOWN)
    up_sum, down_sum = send(added(p10, up), UP), send(added(p31, down), DOWN)
    side = send(added(p01, up_free, down_sum), SIDE)
    return [(p00, 0), (up_sum, 0), (down_free, 0), (side, 0)], [t[8:] for t in (p00, up_sum, down_free, side)]


def reduce_side_first(parts):
    leaving, staying = parts
    side = send(leaving, SIDE)

    def row(dx, half):
        rows = slice(dx * 16 + half * 8, dx * 16 + half * 8 + 8)
        return staying[rows], side[rows]

    up, down = send(added(*row(2, 0)), UP), send(added(*row(2, 1)), DOWN)
    up_free, down_free = send(added(*row(1, 1)), UP), send(added(*row(3, 0)), DOWN)
    up_sum, down_sum = send(added(*row(1, 0), up), UP), send(added(*row(3, 1), down), DOWN)
    own = [(staying, 0), (side, 0), (up_sum, 0), (down_free, 0)]
    return own, [staying[8:16], side[8:16], up_free, down_sum]


def gather_side_first(rows):
    side = send(rows, SIDE)
    low0, high0 = send(rows, UP), send(rows, DOWN)
    low1, high1 = send(side, UP), send(side, DOWN)
    far0, far1 = send(low0, UP), send(high1, DOWN)
    return [rows, side, high0, high1, far0, far1, low0, low1]


def gather_side_last(rows):
    low, high = send(rows, UP), send(rows, DOWN)
    far0, far1 = send(low[:8], UP), send(high[8:], DOWN)
    rows_s, low_s, high_s = send(rows, SIDE), send(low, SIDE), send(high, SIDE)
    far0_s, far1_s = send(far0, SIDE), send(far1, SIDE)
    return [rows, rows_s, high, high_s, far0, far1, far0_s, far1_s, low, low_s]


SIDE_LAST_GROUPS = ((64,), (80,), (32,), (48,), (96,), (112,), (0,), (16,))
SIDE_FIRST_GROUPS = ((16, 48, 80, 112), (0, 32, 64, 96))


def on_device(cholesky, fields, orbitals, cotangent):
    vec_rows, columns = cholesky.shape
    walkers = fields.shape[1]
    width = orbitals.shape[2]
    chunk_width = columns // (2 * CHUNKS)
    depth = chunk_width // width
    pair, walk = lax.axis_index("pair"), lax.axis_index("walk")
    z, yh = pair // 2, pair % 2
    x, yl, c = walk // 4, (walk // 2) % 2, walk % 2
    at = jnp.reshape(c, (1,)).astype(jnp.int32)

    r = lax.broadcasted_iota(jnp.int32, (walkers, walkers), 1)
    dx, dyl, dc, m, dz = r // 32, (r // 16) % 2, (r // 8) % 2, (r // 4) % 2, r % 4
    walker_z, walker_yh = (z + dz) % 4, (yh + m) % 2
    walker_x, walker_yl, walker_c = (x + dx) % 4, (yl + dyl + m) % 2, (c + dc) % 2
    walker = (walker_z * 2 + walker_yh) * 16 + walker_x * 4 + walker_yl * 2 + walker_c
    order = lax.broadcasted_iota(jnp.int32, (walkers, walkers), 0) == walker
    fields_here = jnp.concatenate(
        [
            lax.dynamic_slice_in_dim(fields, walk * vec_rows, vec_rows, 0),
            lax.dynamic_slice_in_dim(fields, (walk + 1 - 2 * c) * vec_rows, vec_rows, 0),
        ],
        axis=0,
    )
    fields_rel = jnp.dot(fields_here, order.astype(BF16), preferred_element_type=F32).astype(BF16)
    fields_turned = lax.dot_general(
        order.astype(BF16), fields_here, (((0,), (1,)), ((), ())), preferred_element_type=F32
    ).astype(BF16)

    others, blocks = [], []
    for chunk in range(CHUNKS):
        leaving = lax.dynamic_slice(
            cholesky, (0, (1 - c) * (columns // 2) + chunk * chunk_width), (vec_rows, chunk_width)
        )
        others.append(send(leaving, CORE))
    for chunk in range(CHUNKS):
        side_first = chunk == 0
        groups = SIDE_FIRST_GROUPS if side_first else SIDE_LAST_GROUPS
        parts = partial_sums(at, fields_turned, cholesky, others[chunk], chunk, groups)
        own, crossing = (reduce_side_first if side_first else reduce_side_last)(parts)
        crossed = send(added(*crossing), CORE)
        out = unpack([array for array, _ in own], crossed, width)
        blocks += [out[0]] + [send(out[i], across(*OTHERS[i])) for i in range(1, 8)]

    def block_row(z_at, yh_at, half, chunk):
        return (z_at * 2 + yh_at) * (columns // width) + (c + half) % 2 * (columns // width // 2) + chunk * depth

    rows_in = [
        block_row((z + 4 - dz) % 4, (yh + m) % 2, half, chunk)
        for chunk in range(CHUNKS)
        for m, dz in OTHERS
        for half in range(2)
    ]
    rows_out = [
        block_row((z + dz) % 4, (yh + m) % 2, half, chunk)
        for chunk in range(CHUNKS)
        for m, dz in OTHERS
        for half in range(2)
    ]
    orbit_grad, *leaving = taylor(jnp.stack(rows_in + rows_out).astype(jnp.int32), orbitals, cotangent, blocks)

    field = jnp.zeros((2 * vec_rows, walkers), F32)
    chol_grad = None
    for chunk in range(CHUNKS):
        arrived = [leaving[chunk * 8]] + [send(leaving[chunk * 8 + i], across(*OTHERS[i])) for i in range(1, 8)]
        own, crossing = pack([arrived[m * 4 + (4 - dz) % 4] for m, dz in OTHERS])
        rows = jnp.concatenate([own, send(crossing, CORE)], axis=0)
        parts = (gather_side_last if chunk == 0 else gather_side_first)(rows)
        chol_grad, other, field = finish(
            at, fields_rel, cholesky, others[chunk], field, parts, chunk, chol_grad
        )
        chol_grad = place(at, send(other, CORE), chol_grad, chunk)

    natural = lax.dot_general(
        field, order.astype(F32), (((1,), (1,)), ((), ())), precision=lax.Precision.HIGHEST, preferred_element_type=F32
    )
    summed = natural[:vec_rows] + send(natural[vec_rows:].astype(BF16), CORE).astype(F32)
    n_pair = lax.axis_size("pair")
    apart = summed.astype(BF16).reshape(vec_rows, n_pair, walkers // n_pair).transpose(1, 0, 2)
    field_grad = lax.all_to_all(apart, "pair", split_axis=0, concat_axis=0, tiled=True).astype(F32).sum(axis=0)
    return (orbit_grad, chol_grad, field_grad)


def solution(mesh):
    in_specs = (
        P("walk", "pair"),
        P(),
        P(("pair", "walk"), None, None),
        P(("pair", "walk"), None, None),
    )
    out_specs = (P(("pair", "walk"), None, None), P("walk", "pair"), P("walk", "pair"))
    return jax.shard_map(
        on_device, mesh=mesh, in_specs=in_specs, out_specs=out_specs, check_vma=False
    )
```

```python
import functools

import jax
import jax.numpy as jnp
from jax import lax
from jax.experimental import pallas as pl
from jax.experimental.pallas import tpu as pltpu
from jax.sharding import PartitionSpec as P


BF16 = jnp.bfloat16
F32 = jnp.float32
ALL = ("pair", "walk")
CHUNKS = 3
REDUCED = (1, 0, 2)
LAST = (("finish", 1), ("finish", 0), ("place", 1), ("place", 0), ("finish", 2), ("place", 2))
BLOCK = 4096
PLACE = 6144
LANES = 128


def moved(to):
    pairs = []
    for z in range(4):
        for yh in range(2):
            for x in range(4):
                for yl in range(2):
                    for c in range(2):
                        z2, yh2, x2, yl2, c2 = to(z, yh, x, yl, c)
                        here = ((z * 2 + yh) * 4 + x) * 4 + yl * 2 + c
                        there = (((z2 % 4) * 2 + yh2 % 2) * 4 + x2 % 4) * 4 + (yl2 % 2) * 2 + c2 % 2
                        pairs.append((here, there))
    return pairs


CORE = moved(lambda z, yh, x, yl, c: (z, yh, x, yl, c + 1))
SIDE = moved(lambda z, yh, x, yl, c: (z, yh, x, yl + 1, c))
UP = moved(lambda z, yh, x, yl, c: (z, yh, x + 1, yl, c))
DOWN = moved(lambda z, yh, x, yl, c: (z, yh, x + 3, yl, c))
OTHERS = [(m, dz) for m in range(2) for dz in range(4)]


def across(m, dz):
    return moved(lambda z, yh, x, yl, c: (z + dz, yh + m, x, yl + m, c))


def send(array, pairs):
    return lax.ppermute(array, ALL, pairs)


def tied(array, *others):
    return lax.optimization_barrier((array, *others))[0]


def added(*terms):
    total = terms[0].astype(F32)
    for term in terms[1:]:
        total = total + term.astype(F32)
    return total.astype(BF16)


def whole(shape):
    return pl.BlockSpec(shape, lambda *_: (0,) * len(shape))


def partial_kernel(groups, at_ref, weights_ref, own_ref, other_ref, after_ref, *outs):
    rows = jnp.concatenate([own_ref[...], other_ref[...]], axis=0)
    sums = jnp.dot(weights_ref[...], rows, preferred_element_type=F32).astype(BF16)
    for group, out in zip(groups, outs):
        for place, start in enumerate(group):
            out[place * 16 : place * 16 + 16, :] = sums[start : start + 16]


def partial_sums(at, weights, cholesky, other, chunk, groups, after):
    rows, width = other.shape
    steps = width // BLOCK
    return pl.pallas_call(
        functools.partial(partial_kernel, groups),
        grid_spec=pltpu.PrefetchScalarGridSpec(
            num_scalar_prefetch=1,
            grid=(steps,),
            in_specs=[
                whole(weights.shape),
                pl.BlockSpec((rows, BLOCK), lambda i, at: (0, at[0] * (CHUNKS * steps) + chunk * steps + i)),
                pl.BlockSpec((rows, BLOCK), lambda i, at: (0, i)),
                pl.BlockSpec(memory_space=pl.ANY),
            ],
            out_specs=[pl.BlockSpec((16 * len(g), BLOCK), lambda i, at: (0, i)) for g in groups],
        ),
        out_shape=[jax.ShapeDtypeStruct((16 * len(g), width), BF16) for g in groups],
        cost_estimate=pl.CostEstimate(flops=2 * 128 * 128 * width, bytes_accessed=512 * width, transcendentals=0),
        name="partial_sums",
    )(at, weights, cholesky, other, after)


def unpack_kernel(depth, width, n_own, has_outs, *refs):
    own, other = refs[:n_own], refs[n_own : n_own + 1]
    outs, scratch = refs[n_own + 1 + 8 * has_outs : -1], refs[-1]
    across_lanes = width // LANES
    for half, parts in enumerate((own, other)):
        for tile in range(depth * across_lanes):
            lanes = slice(tile * LANES, (tile + 1) * LANES)
            total = parts[0][0:8, lanes].astype(F32)
            for part in parts[1:]:
                total = total + part[0:8, lanes].astype(F32)
            scratch[half, tile * 8 : tile * 8 + 8, :] = total
        for walker in range(8):
            for lane in range(across_lanes):
                tall = [
                    scratch[half, pl.ds((top * across_lanes + lane) * 8 + walker, 8, stride=8 * across_lanes), :]
                    for top in range(0, depth, 8)
                ]
                outs[walker][half, :, lane * LANES : (lane + 1) * LANES] = jnp.concatenate(tall, axis=0).astype(BF16)


def unpack(own, other, chunk, width, outs):
    depth = other.shape[1] // width
    arrays = [*own, other]
    specs = [pl.BlockSpec((8, depth * width), lambda i: (0, 0)) for _ in arrays]
    aliases = {}
    if outs:
        aliases = {len(arrays) + n: n for n in range(8)}
        arrays += outs
        specs += [pl.BlockSpec(memory_space=pl.ANY)] * 8
    return pl.pallas_call(
        functools.partial(unpack_kernel, depth, width, len(own), int(bool(outs))),
        grid=(1,),
        in_specs=specs,
        out_specs=[pl.BlockSpec((2, depth, width), lambda i: (0, chunk, 0)) for _ in OTHERS],
        out_shape=[jax.ShapeDtypeStruct((2, CHUNKS * depth, width), BF16) for _ in OTHERS],
        scratch_shapes=[pltpu.VMEM((2, depth * width // LANES * 8, LANES), F32)],
        input_output_aliases=aliases,
        name="unpack",
    )(*arrays)


def pack_kernel(depth, width, *refs):
    blocks, own, other, scratch = refs[:8], refs[8], refs[9], refs[10]
    across_lanes = width // LANES
    for half, out in enumerate((own, other)):
        for walker in range(8):
            for lane in range(across_lanes):
                tall = blocks[walker][half, :, lane * LANES : (lane + 1) * LANES].astype(F32)
                for top in range(0, depth, 8):
                    rows = pl.ds((top * across_lanes + lane) * 8 + walker, 8, stride=8 * across_lanes)
                    scratch[half, rows, :] = tall[top : top + 8]
        for tile in range(depth * across_lanes):
            out[:, tile * LANES : (tile + 1) * LANES] = scratch[half, tile * 8 : tile * 8 + 8, :].astype(BF16)


def pack(blocks, chunk, after):
    _, rows, width = blocks[0].shape
    depth = rows // CHUNKS
    return pl.pallas_call(
        lambda *refs: pack_kernel(depth, width, *refs[:8], *refs[9:]),
        grid=(1,),
        in_specs=[pl.BlockSpec((2, depth, width), lambda i: (0, chunk, 0)) for _ in blocks]
        + [pl.BlockSpec(memory_space=pl.ANY)],
        out_specs=[whole((8, depth * width))] * 2,
        out_shape=[jax.ShapeDtypeStruct((8, depth * width), BF16)] * 2,
        scratch_shapes=[pltpu.VMEM((2, depth * width // LANES * 8, LANES), F32)],
        name="pack",
    )(*blocks, after)


def taylor_kernel(n_blocks, depths, at_ref, orbit_ref, cotan_ref, *refs):
    blocks, orbit_out, outs = refs[:n_blocks], refs[n_blocks], refs[n_blocks + 1 : 2 * n_blocks + 1]
    matrix, grad, series, adjoint = refs[2 * n_blocks + 1 :]
    width = matrix.shape[0]
    tile = 256
    for n, block in enumerate(blocks):
        for half in range(2):
            row = pl.multiple_of(at_ref[2 * n + half], 16)
            matrix[pl.ds(row, depths[n]), :] = block[half]
    series[0] = orbit_ref[0]
    adjoint[4] = cotan_ref[0]

    def tiles(body):
        def step(i, carry):
            body(pl.ds(pl.multiple_of(i * tile, tile), tile))
            return carry

        lax.fori_loop(0, width // tile, step, 0)

    for degree in (1, 2, 3):
        down = 4 - degree

        def both(at, degree=degree, down=down):
            product = lax.dot_general(
                series[degree - 1], matrix[at, :], (((1,), (1,)), ((), ())), preferred_element_type=F32
            )
            series[degree, :, at] = (product / degree).astype(BF16)
            product = jnp.dot(adjoint[down + 1], matrix[:, at], preferred_element_type=F32)
            adjoint[down, :, at] = (cotan_ref[0, :, at].astype(F32) + product / (down + 1)).astype(BF16)

        tiles(both)

    def last(at):
        product = jnp.dot(adjoint[1], matrix[:, at], preferred_element_type=F32)
        orbit_out[0, :, at] = (cotan_ref[0, :, at].astype(F32) + product).astype(BF16)
        total = None
        for degree in range(1, 5):
            term = lax.dot_general(
                adjoint[degree, :, at], series[degree - 1], (((0,), (0,)), ((), ())), preferred_element_type=F32
            )
            total = term if total is None else total + term / degree
        grad[at, :] = total.astype(BF16)

    tiles(last)
    for n, out in enumerate(outs):
        for half in range(2):
            row = pl.multiple_of(at_ref[2 * n_blocks + 2 * n + half], 16)
            out[half] = grad[pl.ds(row, depths[n]), :]


def taylor(at, orbitals, cotangent, blocks):
    width = orbitals.shape[2]
    n = len(blocks)
    specs = [whole(block.shape) for block in blocks]
    return pl.pallas_call(
        functools.partial(taylor_kernel, n, [block.shape[1] for block in blocks]),
        grid_spec=pltpu.PrefetchScalarGridSpec(
            num_scalar_prefetch=1,
            grid=(1,),
            in_specs=[whole(orbitals.shape), whole(cotangent.shape)] + specs,
            out_specs=[whole(orbitals.shape)] + specs,
            scratch_shapes=[
                pltpu.VMEM((width, width), BF16),
                pltpu.VMEM((width, width), BF16),
                pltpu.VMEM((4, orbitals.shape[1], width), BF16),
                pltpu.VMEM((5, orbitals.shape[1], width), BF16),
            ],
        ),
        out_shape=[jax.ShapeDtypeStruct(orbitals.shape, BF16)]
        + [jax.ShapeDtypeStruct(block.shape, BF16) for block in blocks],
        name="taylor",
    )(at, orbitals, cotangent, *blocks)


def finish_kernel(n_parts, has_out, at_ref, weights_ref, own_ref, other_ref, field_ref, *refs):
    parts = refs[:n_parts]
    chol_out, other_out, field_out = refs[n_parts + has_out :]

    @pl.when(pl.program_id(0) == 0)
    def _():
        field_out[...] = field_ref[...]

    grads = jnp.concatenate([part[...] for part in parts], axis=0)
    rows = jnp.concatenate([own_ref[...], other_ref[...]], axis=0)
    field_out[...] += lax.dot_general(rows, grads, (((1,), (1,)), ((), ())), preferred_element_type=F32)
    total = jnp.dot(weights_ref[...], grads, preferred_element_type=F32).astype(BF16)
    half = total.shape[0] // 2
    chol_out[...] = total[:half]
    other_out[...] = total[half:]


def finish(at, weights, cholesky, other, field, parts, chunk, out):
    rows, width = other.shape
    steps = width // BLOCK
    here = pl.BlockSpec((rows, BLOCK), lambda i, at: (0, at[0] * (CHUNKS * steps) + chunk * steps + i))
    in_specs = [whole(weights.shape), here, pl.BlockSpec((rows, BLOCK), lambda i, at: (0, i)), whole(field.shape)]
    for part in parts:
        array, row = part if isinstance(part, tuple) else (part, None)
        height = array.shape[0] if row is None else 16
        in_specs.append(pl.BlockSpec((height, BLOCK), lambda i, at, row=row or 0: (row, i)))
    parts = [part[0] if isinstance(part, tuple) else part for part in parts]
    args = [at, weights, cholesky, other, field, *parts]
    aliases = {}
    if out is not None:
        aliases = {len(args): 0}
        args.append(out)
        in_specs.append(pl.BlockSpec(memory_space=pl.ANY))
    return pl.pallas_call(
        functools.partial(finish_kernel, len(parts), int(out is not None)),
        grid_spec=pltpu.PrefetchScalarGridSpec(
            num_scalar_prefetch=1,
            grid=(steps,),
            in_specs=in_specs,
            out_specs=[here, pl.BlockSpec((rows, BLOCK), lambda i, at: (0, i)), whole(field.shape)],
        ),
        out_shape=[
            jax.ShapeDtypeStruct(cholesky.shape, BF16),
            jax.ShapeDtypeStruct((rows, width), BF16),
            jax.ShapeDtypeStruct(field.shape, F32),
        ],
        input_output_aliases=aliases,
        cost_estimate=pl.CostEstimate(flops=4 * 128 * 128 * width, bytes_accessed=768 * width, transcendentals=0),
        name="finish",
    )(*args)


def place_kernel(at_ref, piece_ref, out_in, out_ref):
    out_ref[...] = piece_ref[...]


def place(at, piece, out, chunk):
    rows, width = piece.shape
    steps = width // PLACE
    return pl.pallas_call(
        place_kernel,
        grid_spec=pltpu.PrefetchScalarGridSpec(
            num_scalar_prefetch=1,
            grid=(steps,),
            in_specs=[pl.BlockSpec((rows, PLACE), lambda i, at: (0, i)), pl.BlockSpec(memory_space=pl.ANY)],
            out_specs=pl.BlockSpec((rows, PLACE), lambda i, at: (0, (1 - at[0]) * (CHUNKS * steps) + chunk * steps + i)),
        ),
        out_shape=jax.ShapeDtypeStruct(out.shape, out.dtype),
        input_output_aliases={2: 0},
        name="place",
    )(at, piece, out)


def reduce_side_last(parts, tie):
    far_up, far_down, near_up, near_down, here0, here1 = parts
    up, down = send(far_up, UP), send(far_down, DOWN)
    up = send(jnp.concatenate([added(near_up[:16], up), near_up[16:]], axis=0), UP)
    down = send(jnp.concatenate([near_down[:16], added(near_down[16:], down)], axis=0), DOWN)
    side = send(added(tied(here1, tie), up[16:], down[16:]), SIDE)
    return [here0, up, down, side], [t[8:16] for t in (here0, up, down, side)]


def reduce_side_first(parts):
    leaving, staying = parts
    side = send(leaving, SIDE)

    def row(dx, half):
        rows = slice(dx * 16 + half * 8, dx * 16 + half * 8 + 8)
        return staying[rows], side[rows]

    far_up, far_down = added(*row(2, 0)), added(*row(2, 1))
    up, down = send(far_up, UP), send(far_down, DOWN)
    near_up = jnp.concatenate([added(*row(1, 0), up), added(*row(1, 1))], axis=0)
    near_down = jnp.concatenate([added(*row(3, 0)), added(*row(3, 1), down)], axis=0)
    up, down = send(near_up, UP), send(near_down, DOWN)
    return [staying, side, up, down], [t[8:16] for t in (staying, side, up, down)], (far_down, near_down)


def gather_side_first(rows):
    rows = jnp.concatenate([rows, send(rows, SIDE)], axis=0)
    low, high = send(rows, UP), send(rows, DOWN)
    far0, far1 = send(low[:16], UP), send(high[16:], DOWN)
    return [rows, high, far0, far1, low]


def gather_side_last(rows):
    low, high = send(rows, UP), send(rows, DOWN)
    far0, far1 = send(low[:8], UP), send(high[8:], DOWN)
    rows_s = send(rows, SIDE)
    near_s = send(jnp.concatenate([high, low], axis=0), SIDE)
    far_s = send(jnp.concatenate([far0, far1], axis=0), SIDE)
    return [rows, rows_s, (high, 0), (near_s, 0), far0, far1, far_s, (low, 0), (near_s, 1)]


SIDE_LAST_GROUPS = ((64,), (80,), (32, 48), (96, 112), (0,), (16,))
SIDE_FIRST_GROUPS = ((16, 48, 80, 112), (0, 32, 64, 96))


def on_device(cholesky, fields, orbitals, cotangent):
    vec_rows, columns = cholesky.shape
    walkers = fields.shape[1]
    width = orbitals.shape[2]
    chunk_width = columns // (2 * CHUNKS)
    pair, walk = lax.axis_index("pair"), lax.axis_index("walk")
    z, yh = pair // 2, pair % 2
    x, yl, c = walk // 4, (walk // 2) % 2, walk % 2
    at = jnp.reshape(c, (1,)).astype(jnp.int32)

    r = lax.broadcasted_iota(jnp.int32, (walkers, walkers), 1)
    dx, dyl, dc, m, dz = r // 32, (r // 16) % 2, (r // 8) % 2, (r // 4) % 2, r % 4
    walker_z, walker_yh = (z + dz) % 4, (yh + m) % 2
    walker_x, walker_yl, walker_c = (x + dx) % 4, (yl + dyl + m) % 2, (c + dc) % 2
    walker = (walker_z * 2 + walker_yh) * 16 + walker_x * 4 + walker_yl * 2 + walker_c
    order = lax.broadcasted_iota(jnp.int32, (walkers, walkers), 0) == walker
    fields_here = jnp.concatenate(
        [
            lax.dynamic_slice_in_dim(fields, walk * vec_rows, vec_rows, 0),
            lax.dynamic_slice_in_dim(fields, (walk + 1 - 2 * c) * vec_rows, vec_rows, 0),
        ],
        axis=0,
    )
    fields_rel = jnp.dot(fields_here, order.astype(BF16), preferred_element_type=F32).astype(BF16)
    fields_turned = lax.dot_general(
        order.astype(BF16), fields_here, (((0,), (1,)), ((), ())), preferred_element_type=F32
    ).astype(BF16)

    others = []
    for chunk in range(CHUNKS):
        leaving = lax.dynamic_slice(
            cholesky if chunk == 0 else tied(cholesky, fields_turned),
            (0, (1 - c) * (columns // 2) + chunk * chunk_width),
            (vec_rows, chunk_width),
        )
        others.append(send(leaving, CORE))
    sums, after, ties = [], fields_turned, None
    for chunk in range(CHUNKS):
        groups = SIDE_FIRST_GROUPS if chunk == 0 else SIDE_LAST_GROUPS
        parts = partial_sums(at, fields_turned, cholesky, others[chunk], chunk, groups, after)
        after = parts[0]
        if chunk == 0:
            *both, ties = reduce_side_first(parts)
        else:
            both = reduce_side_last(parts, ties[chunk - 1])
        sums.append(both)
    tall = []
    for chunk in REDUCED:
        crossed = send(added(*sums[chunk][1]), CORE)
        tall = unpack(sums[chunk][0], crossed, chunk, width, list(tall))
    blocks = [tall[0]] + [send(tall[i], across(*OTHERS[i])) for i in range(1, 8)]

    def block_row(z_at, yh_at, half):
        return (z_at * 2 + yh_at) * (columns // width) + (c + half) % 2 * (columns // width // 2)

    rows_in = [block_row((z + 4 - dz) % 4, (yh + m) % 2, half) for m, dz in OTHERS for half in range(2)]
    rows_out = [block_row((z + dz) % 4, (yh + m) % 2, half) for m, dz in OTHERS for half in range(2)]
    orbit_grad, *leaving = taylor(jnp.stack(rows_in + rows_out).astype(jnp.int32), orbitals, cotangent, blocks)

    arrived = [leaving[0]] + [send(leaving[i], across(*OTHERS[i])) for i in range(1, 8)]
    arrived = [arrived[m * 4 + (4 - dz) % 4] for m, dz in OTHERS]
    gathered, after = [], arrived[0]
    for chunk in range(CHUNKS):
        own, crossing = pack(arrived, chunk, after)
        after = own
        rows = jnp.concatenate([own, send(crossing, CORE)], axis=0)
        gathered.append(gather_side_last(rows) if chunk == 0 else gather_side_first(rows))
    field = jnp.zeros((2 * vec_rows, walkers), F32)
    chol_grad = None
    leaving = {}
    for kind, chunk in LAST:
        if kind == "finish":
            chol_grad, other, field = finish(
                at, fields_rel, cholesky, others[chunk], field, gathered[chunk], chunk, chol_grad
            )
            leaving[chunk] = send(other, CORE)
        else:
            chol_grad = place(at, leaving[chunk], chol_grad, chunk)

    natural = lax.dot_general(
        field, order.astype(F32), (((1,), (1,)), ((), ())), precision=lax.Precision.HIGHEST, preferred_element_type=F32
    )
    summed = natural[:vec_rows] + send(natural[vec_rows:].astype(BF16), CORE).astype(F32)
    n_pair = lax.axis_size("pair")
    apart = summed.astype(BF16).reshape(vec_rows, n_pair, walkers // n_pair).transpose(1, 0, 2)
    field_grad = lax.all_to_all(apart, "pair", split_axis=0, concat_axis=0, tiled=True).astype(F32).sum(axis=0)
    return (orbit_grad, chol_grad, field_grad)


def solution(mesh):
    in_specs = (
        P("walk", "pair"),
        P(),
        P(("pair", "walk"), None, None),
        P(("pair", "walk"), None, None),
    )
    out_specs = (P(("pair", "walk"), None, None), P("walk", "pair"), P("walk", "pair"))

    return jax.shard_map(on_device, mesh=mesh, in_specs=in_specs, out_specs=out_specs, check_vma=False)
```

```python
import functools

import jax
import jax.numpy as jnp
from jax import lax
from jax.experimental import pallas as pl
from jax.experimental.pallas import tpu as pltpu
from jax.sharding import PartitionSpec as P


BF16 = jnp.bfloat16
F32 = jnp.float32
ALL = ("pair", "walk")
CHUNKS = 3
REDUCED = (1, 0, 2)
SUMMED = (1, 0, 2)
PACKED = (1, 0, 2)
FINISHED = (0, 1, 2)
BLOCK = 4096
PLACED = 4
LANES = 128
VMEM = pl.BlockSpec(memory_space=pltpu.VMEM)


def moved(to):
    pairs = []
    for z in range(4):
        for yh in range(2):
            for x in range(4):
                for yl in range(2):
                    for c in range(2):
                        z2, yh2, x2, yl2, c2 = to(z, yh, x, yl, c)
                        here = ((z * 2 + yh) * 4 + x) * 4 + yl * 2 + c
                        there = (((z2 % 4) * 2 + yh2 % 2) * 4 + x2 % 4) * 4 + (yl2 % 2) * 2 + c2 % 2
                        pairs.append((here, there))
    return pairs


CORE = moved(lambda z, yh, x, yl, c: (z, yh, x, yl, c + 1))
SIDE = moved(lambda z, yh, x, yl, c: (z, yh, x, yl + 1, c))
UP = moved(lambda z, yh, x, yl, c: (z, yh, x + 1, yl, c))
DOWN = moved(lambda z, yh, x, yl, c: (z, yh, x + 3, yl, c))
OTHERS = [(m, dz) for m in range(2) for dz in range(4)]


def across(m, dz):
    return moved(lambda z, yh, x, yl, c: (z + dz, yh + m, x, yl + m, c))


def send(array, pairs):
    return lax.ppermute(array, ALL, pairs)


def tied(array, *others):
    return lax.optimization_barrier((array, *others))[0]


def added(*terms):
    total = terms[0].astype(F32)
    for term in terms[1:]:
        total = total + term.astype(F32)
    return total.astype(BF16)


def whole(shape):
    return pl.BlockSpec(shape, lambda *_: (0,) * len(shape))


def take_kernel(start, step, at_ref, all_ref, out_ref, sems):
    column = pl.multiple_of((1 - at_ref[0]) * step + start, LANES)
    copies = []
    for n in range(out_ref.shape[0] // 16):
        rows = slice(16 * n, 16 * n + 16)
        copies.append(
            pltpu.make_async_copy(all_ref.at[rows, pl.ds(column, out_ref.shape[1])], out_ref.at[rows, :], sems.at[n])
        )
    for copy in copies:
        copy.start()
    for copy in copies:
        copy.wait()


def take(at, cholesky, chunk, chunk_width):
    rows = cholesky.shape[0]
    return pl.pallas_call(
        functools.partial(take_kernel, chunk * chunk_width, CHUNKS * chunk_width),
        grid_spec=pltpu.PrefetchScalarGridSpec(
            num_scalar_prefetch=1,
            grid=(1,),
            in_specs=[pl.BlockSpec(memory_space=pl.ANY)],
            out_specs=VMEM,
            scratch_shapes=[pltpu.SemaphoreType.DMA((rows // 16,))],
        ),
        out_shape=jax.ShapeDtypeStruct((rows, chunk_width), BF16),
        name="take",
    )(at, cholesky)


def partial_kernel(groups, at_ref, weights_ref, own_ref, other_ref, after_ref, *outs):
    here = pl.ds(pl.multiple_of(pl.program_id(0) * BLOCK, BLOCK), BLOCK)
    rows = jnp.concatenate([own_ref[...], other_ref[:, here]], axis=0)
    sums = jnp.dot(weights_ref[...], rows, preferred_element_type=F32).astype(BF16)
    for group, out in zip(groups, outs):
        for place, start in enumerate(group):
            out[place * 16 : place * 16 + 16, :] = sums[start : start + 16]


def partial_sums(at, weights, cholesky, other, chunk, groups, after):
    rows, width = other.shape
    steps = width // BLOCK
    return pl.pallas_call(
        functools.partial(partial_kernel, groups),
        grid_spec=pltpu.PrefetchScalarGridSpec(
            num_scalar_prefetch=1,
            grid=(steps,),
            in_specs=[
                whole(weights.shape),
                pl.BlockSpec((rows, BLOCK), lambda i, at: (0, at[0] * (CHUNKS * steps) + chunk * steps + i)),
                VMEM,
                pl.BlockSpec(memory_space=pl.ANY),
            ],
            out_specs=[pl.BlockSpec((16 * len(g), BLOCK), lambda i, at: (0, i)) for g in groups],
        ),
        out_shape=[jax.ShapeDtypeStruct((16 * len(g), width), BF16) for g in groups],
        cost_estimate=pl.CostEstimate(flops=2 * 128 * 128 * width, bytes_accessed=512 * width, transcendentals=0),
        name="partial_sums",
    )(at, weights, cholesky, other, after)


def unpack_kernel(depth, width, n_own, has_outs, *refs):
    own, other = refs[:n_own], refs[n_own : n_own + 1]
    outs, scratch = refs[n_own + 1 + 8 * has_outs : -1], refs[-1]
    across_lanes = width // LANES
    for half, parts in enumerate((own, other)):
        for tile in range(depth * across_lanes):
            lanes = slice(tile * LANES, (tile + 1) * LANES)
            total = parts[0][0:8, lanes].astype(F32)
            for part in parts[1:]:
                total = total + part[0:8, lanes].astype(F32)
            scratch[half, tile * 8 : tile * 8 + 8, :] = total
        for walker in range(8):
            for lane in range(across_lanes):
                tall = [
                    scratch[half, pl.ds((top * across_lanes + lane) * 8 + walker, 8, stride=8 * across_lanes), :]
                    for top in range(0, depth, 8)
                ]
                block = jnp.concatenate(tall, axis=0).astype(BF16)
                outs[walker][half, :, lane * LANES : (lane + 1) * LANES] = block


def unpack(own, other, chunk, width, outs):
    depth = other.shape[1] // width
    arrays = [*own, other]
    specs = [pl.BlockSpec((8, depth * width), lambda i: (0, 0)) for _ in arrays]
    aliases = {}
    if outs:
        aliases = {len(arrays) + n: n for n in range(8)}
        arrays += outs
        specs += [pl.BlockSpec(memory_space=pl.ANY)] * 8
    return pl.pallas_call(
        functools.partial(unpack_kernel, depth, width, len(own), int(bool(outs))),
        grid=(1,),
        in_specs=specs,
        out_specs=[pl.BlockSpec((2, depth, width), lambda i: (0, chunk, 0)) for _ in OTHERS],
        out_shape=[jax.ShapeDtypeStruct((2, CHUNKS * depth, width), BF16) for _ in OTHERS],
        scratch_shapes=[pltpu.VMEM((2, depth * width // LANES * 8, LANES), F32)],
        input_output_aliases=aliases,
        name="unpack",
    )(*arrays)


def pack_kernel(chunk, depth, width, *refs):
    blocks, own, other, scratch = refs[:8], refs[8], refs[9], refs[10]
    across_lanes = width // LANES
    for half, out in enumerate((own, other)):
        for walker in range(8):
            for lane in range(across_lanes):
                tall = blocks[walker][half, chunk * depth : (chunk + 1) * depth, lane * LANES : (lane + 1) * LANES]
                tall = tall.astype(F32)
                for top in range(0, depth, 8):
                    rows = pl.ds((top * across_lanes + lane) * 8 + walker, 8, stride=8 * across_lanes)
                    scratch[half, rows, :] = tall[top : top + 8]
        for tile in range(depth * across_lanes):
            out[:, tile * LANES : (tile + 1) * LANES] = scratch[half, tile * 8 : tile * 8 + 8, :].astype(BF16)


def pack(blocks, chunk, after):
    _, rows, width = blocks[0].shape
    depth = rows // CHUNKS
    return pl.pallas_call(
        lambda *refs: pack_kernel(chunk, depth, width, *refs[:8], *refs[9:]),
        grid=(1,),
        in_specs=[VMEM] * 8 + [pl.BlockSpec(memory_space=pl.ANY)],
        out_specs=[VMEM] * 2,
        out_shape=[jax.ShapeDtypeStruct((8, depth * width), BF16)] * 2,
        scratch_shapes=[pltpu.VMEM((2, depth * width // LANES * 8, LANES), F32)],
        name="pack",
    )(*blocks, after)


def taylor_kernel(n_blocks, depths, at_ref, orbit_ref, cotan_ref, *refs):
    blocks, orbit_out, outs = refs[:n_blocks], refs[n_blocks], refs[n_blocks + 1 : 2 * n_blocks + 1]
    matrix, grad, series, adjoint = refs[2 * n_blocks + 1 :]
    width = matrix.shape[0]
    tile = 256
    for n, block in enumerate(blocks):
        for half in range(2):
            row = pl.multiple_of(at_ref[2 * n + half], 16)
            matrix[pl.ds(row, depths[n]), :] = block[half]
    series[0] = orbit_ref[0]
    adjoint[4] = cotan_ref[0]

    def tiles(body):
        def step(i, carry):
            body(pl.ds(pl.multiple_of(i * tile, tile), tile))
            return carry

        lax.fori_loop(0, width // tile, step, 0)

    for degree in (1, 2, 3):
        down = 4 - degree

        def both(at, degree=degree, down=down):
            product = lax.dot_general(
                series[degree - 1], matrix[at, :], (((1,), (1,)), ((), ())), preferred_element_type=F32
            )
            series[degree, :, at] = (product / degree).astype(BF16)
            product = jnp.dot(adjoint[down + 1], matrix[:, at], preferred_element_type=F32)
            adjoint[down, :, at] = (cotan_ref[0, :, at].astype(F32) + product / (down + 1)).astype(BF16)

        tiles(both)

    def last(at):
        product = jnp.dot(adjoint[1], matrix[:, at], preferred_element_type=F32)
        orbit_out[0, :, at] = (cotan_ref[0, :, at].astype(F32) + product).astype(BF16)
        total = None
        for degree in range(1, 5):
            term = lax.dot_general(
                adjoint[degree, :, at], series[degree - 1], (((0,), (0,)), ((), ())), preferred_element_type=F32
            )
            total = term if total is None else total + term / degree
        grad[at, :] = total.astype(BF16)

    tiles(last)
    for n, out in enumerate(outs):
        for half in range(2):
            row = pl.multiple_of(at_ref[2 * n_blocks + 2 * n + half], 16)
            out[half] = grad[pl.ds(row, depths[n]), :]


def taylor(at, orbitals, cotangent, blocks):
    width = orbitals.shape[2]
    n = len(blocks)
    specs = [VMEM] * n
    return pl.pallas_call(
        functools.partial(taylor_kernel, n, [block.shape[1] for block in blocks]),
        grid_spec=pltpu.PrefetchScalarGridSpec(
            num_scalar_prefetch=1,
            grid=(1,),
            in_specs=[VMEM, VMEM] + specs,
            out_specs=[VMEM] + specs,
            scratch_shapes=[
                pltpu.VMEM((width, width), BF16),
                pltpu.VMEM((width, width), BF16),
                pltpu.VMEM((4, orbitals.shape[1], width), BF16),
                pltpu.VMEM((5, orbitals.shape[1], width), BF16),
            ],
        ),
        out_shape=[jax.ShapeDtypeStruct(orbitals.shape, BF16)]
        + [jax.ShapeDtypeStruct(block.shape, BF16) for block in blocks],
        name="taylor",
    )(at, orbitals, cotangent, *blocks)


def field_kernel(n_parts, own_ref, other_ref, field_ref, *refs):
    grads = jnp.concatenate([part[...] for part in refs[:n_parts]], axis=0)
    rows = jnp.concatenate([own_ref[...], other_ref[...]], axis=0)
    refs[-1][...] += lax.dot_general(rows, grads, (((1,), (1,)), ((), ())), preferred_element_type=F32)


def chol_kernel(n_parts, weights_ref, *refs):
    grads = jnp.concatenate([part[...] for part in refs[:n_parts]], axis=0)
    total = jnp.dot(weights_ref[...], grads, preferred_element_type=F32).astype(BF16)
    chol_out, other_out = refs[-2:]
    half = total.shape[0] // 2
    chol_out[...] = total[:half]
    other_out[...] = total[half:]


def finish_kernel(n_parts, has_out, do_field, do_chol, at_ref, *refs):
    refs = list(refs)
    weights = [refs.pop(0)] if do_chol else []
    columns = [refs.pop(0) for _ in range(3)] if do_field else []
    parts, refs = refs[:n_parts], refs[n_parts + has_out :]
    if do_field:

        @pl.when(pl.program_id(0) == 0)
        def _():
            refs[-1][...] = columns[2][...]

        field_kernel(n_parts, *columns, *parts, refs[-1])
    if do_chol:
        chol_kernel(n_parts, *weights, *parts, *refs[:2])


def finish(at, weights, cholesky, other, field, parts, chunk, out, do_field=True, do_chol=True):
    rows, width = other.shape
    steps = width // BLOCK
    here = pl.BlockSpec((rows, BLOCK), lambda i, at: (0, at[0] * (CHUNKS * steps) + chunk * steps + i))
    along = pl.BlockSpec((rows, BLOCK), lambda i, at: (0, i))
    args, in_specs, out_specs, out_shape, aliases = [at], [], [], [], {}
    if do_chol:
        args.append(weights)
        in_specs.append(whole(weights.shape))
        out_specs += [here, along]
        out_shape += [jax.ShapeDtypeStruct(cholesky.shape, BF16), jax.ShapeDtypeStruct((rows, width), BF16)]
    if do_field:
        args += [cholesky, other, field]
        in_specs += [here, along, whole(field.shape)]
        out_specs.append(whole(field.shape))
        out_shape.append(jax.ShapeDtypeStruct(field.shape, F32))
    for part in parts:
        array, row = part if isinstance(part, tuple) else (part, None)
        height = array.shape[0] if row is None else 16
        args.append(array)
        in_specs.append(pl.BlockSpec((height, BLOCK), lambda i, at, row=row or 0: (row, i)))
    if do_chol and out is not None:
        aliases = {len(args): 0}
        args.append(out)
        in_specs.append(pl.BlockSpec(memory_space=pl.ANY))
    return pl.pallas_call(
        functools.partial(finish_kernel, len(parts), len(aliases), do_field, do_chol),
        grid_spec=pltpu.PrefetchScalarGridSpec(
            num_scalar_prefetch=1, grid=(steps,), in_specs=in_specs, out_specs=out_specs
        ),
        out_shape=out_shape,
        input_output_aliases=aliases,
        cost_estimate=pl.CostEstimate(flops=4 * 128 * 128 * width, bytes_accessed=768 * width, transcendentals=0),
        name="finish",
    )(*args)


def place_kernel(starts, step, at_ref, *refs):
    pieces, out_ref, sems = refs[: len(starts)], refs[len(starts) + 1], refs[len(starts) + 2]
    copies = []
    for n, (piece, start) in enumerate(zip(pieces, starts)):
        column = pl.multiple_of((1 - at_ref[0]) * step + start, LANES)
        for m in range(PLACED):
            rows = slice(m * piece.shape[0] // PLACED, (m + 1) * piece.shape[0] // PLACED)
            copies.append(
                pltpu.make_async_copy(
                    piece.at[rows, :], out_ref.at[rows, pl.ds(column, piece.shape[1])], sems.at[n * PLACED + m]
                )
            )
    for copy in copies:
        copy.start()
    for copy in copies:
        copy.wait()


def place(at, pieces, out):
    width = pieces[0].shape[1]
    n = len(pieces)
    return pl.pallas_call(
        functools.partial(place_kernel, [chunk * width for chunk in range(n)], n * width),
        grid_spec=pltpu.PrefetchScalarGridSpec(
            num_scalar_prefetch=1,
            grid=(1,),
            in_specs=[VMEM] * n + [pl.BlockSpec(memory_space=pl.ANY)],
            out_specs=pl.BlockSpec(memory_space=pl.ANY),
            scratch_shapes=[pltpu.SemaphoreType.DMA((n * PLACED,))],
        ),
        out_shape=jax.ShapeDtypeStruct(out.shape, out.dtype),
        input_output_aliases={n + 1: 0},
        name="place",
    )(at, *pieces, out)


def merge_kernel(start, near_ref, came_ref, out_ref):
    height = came_ref.shape[0]
    rest = height - start
    out_ref[rest : rest + height, :] = near_ref[rest : rest + height, :]
    out_ref[start : start + height, :] = added(near_ref[start : start + height, :], came_ref[...])


def merge(near, came, start):
    return pl.pallas_call(
        functools.partial(merge_kernel, start),
        in_specs=[VMEM] * 2,
        out_specs=VMEM,
        out_shape=jax.ShapeDtypeStruct(near.shape, BF16),
        name="merge",
    )(near, came)


def reduce_side_last(parts, n, tie):
    up, down = send(parts[0], UP), send(parts[1], DOWN)
    if n == 1:
        near_up, free_up, free_down, near_down, here0, here1 = parts[2:]
        free_up, free_down = send(free_up, UP), send(free_down, DOWN)
        up, down = lax.optimization_barrier((added(near_up, up), added(near_down, down)))
        up, down = send(up, UP), send(down, DOWN)
        side = send(added(tied(here1, tie), free_up, down), SIDE)
        return [here0, up, free_down, side], [t[8:16] for t in (here0, up, free_down, side)]
    near_up, near_down, here0, here1 = parts[2:]
    up = merge(near_up, up, 0)
    down = merge(near_down, down, 16)
    up, down = send(up, UP), send(down, DOWN)
    side = send(added(tied(here1, tie), up[16:], down[16:]), SIDE)
    return [here0, up, down, side], [t[8:16] for t in (here0, up, down, side)]


def reduce_side_first(parts):
    leaving, staying = parts
    side = send(leaving, SIDE)

    def row(dx, half):
        rows = slice(dx * 16 + half * 8, dx * 16 + half * 8 + 8)
        return staying[rows], side[rows]

    far_up, far_down = lax.optimization_barrier((added(*row(2, 0)), added(*row(2, 1))))
    up, down = send(far_up, UP), send(far_down, DOWN)
    near_up = jnp.concatenate([added(*row(1, 0), up), added(*row(1, 1))], axis=0)
    near_down = jnp.concatenate([added(*row(3, 0)), added(*row(3, 1), down)], axis=0)
    up, down = send(near_up, UP), send(near_down, DOWN)
    return [staying, side, up, down], [t[8:16] for t in (staying, side, up, down)], (far_down, near_down)


def gather_side_first(rows):
    rows = jnp.concatenate([rows, send(rows, SIDE)], axis=0)
    low, high = send(rows, UP), send(rows, DOWN)
    far0, far1 = send(low[:16], UP), send(high[16:], DOWN)
    return [rows, high, far0, far1, low]


def gather_side_last(rows):
    low, high = send(rows, UP), send(rows, DOWN)
    far0, far1 = send(low[:8], UP), send(high[8:], DOWN)
    rows_s = send(rows, SIDE)
    near_s = send(jnp.concatenate([high, low], axis=0), SIDE)
    far_s = send(jnp.concatenate([far0, far1], axis=0), SIDE)
    return [rows, rows_s, (high, 0), (near_s, 0), far0, far1, far_s, (low, 0), (near_s, 1)]


SIDE_LAST_GROUPS = ((64,), (80,), (32, 48), (96, 112), (0,), (16,))
FREE_GROUPS = ((64,), (80,), (32,), (48,), (96,), (112,), (0,), (16,))
SIDE_FIRST_GROUPS = ((16, 48, 80, 112), (0, 32, 64, 96))


def summed_of(at, weights, cholesky, others, chunk, after):
    groups = (SIDE_FIRST_GROUPS, FREE_GROUPS, SIDE_LAST_GROUPS)[chunk]
    return partial_sums(at, weights, cholesky, others[chunk], chunk, groups, after)


def on_device(cholesky, fields, orbitals, cotangent):
    vec_rows, columns = cholesky.shape
    walkers = fields.shape[1]
    width = orbitals.shape[2]
    chunk_width = columns // (2 * CHUNKS)
    pair, walk = lax.axis_index("pair"), lax.axis_index("walk")
    z, yh = pair // 2, pair % 2
    x, yl, c = walk // 4, (walk // 2) % 2, walk % 2
    at = jnp.reshape(c, (1,)).astype(jnp.int32)

    r = lax.broadcasted_iota(jnp.int32, (walkers, walkers), 1)
    dx, dyl, dc, m, dz = r // 32, (r // 16) % 2, (r // 8) % 2, (r // 4) % 2, r % 4
    walker_z, walker_yh = (z + dz) % 4, (yh + m) % 2
    walker_x, walker_yl, walker_c = (x + dx) % 4, (yl + dyl + m) % 2, (c + dc) % 2
    walker = (walker_z * 2 + walker_yh) * 16 + walker_x * 4 + walker_yl * 2 + walker_c
    order = lax.broadcasted_iota(jnp.int32, (walkers, walkers), 0) == walker
    fields_here = jnp.concatenate(
        [
            lax.dynamic_slice_in_dim(fields, walk * vec_rows, vec_rows, 0),
            lax.dynamic_slice_in_dim(fields, (walk + 1 - 2 * c) * vec_rows, vec_rows, 0),
        ],
        axis=0,
    )
    fields_rel = jnp.dot(fields_here, order.astype(BF16), preferred_element_type=F32).astype(BF16)
    fields_turned = lax.dot_general(
        order.astype(BF16), fields_here, (((0,), (1,)), ((), ())), preferred_element_type=F32
    ).astype(BF16)

    others, sums, after, ties = [None] * CHUNKS, [None] * CHUNKS, fields_turned, None
    partials = [None] * CHUNKS
    for place_at, chunk in enumerate(SUMMED):
        whole_rows = cholesky if place_at < 2 else tied(cholesky, partials[SUMMED[0]][0])
        leaving = take(at, whole_rows, chunk, chunk_width)
        others[chunk] = send(leaving, CORE)
        if place_at == 1:
            partials[SUMMED[0]] = summed_of(at, fields_turned, cholesky, others, SUMMED[0], fields_turned)
    for last, chunk in zip(SUMMED, SUMMED[1:]):
        partials[chunk] = summed_of(at, fields_turned, cholesky, others, chunk, partials[last][0])
    *sums[0], ties = reduce_side_first(partials[0])
    for chunk in (1, 2):
        sums[chunk] = reduce_side_last(partials[chunk], chunk, ties[chunk - 1])
    tall = []
    for chunk in REDUCED:
        crossed = send(added(*sums[chunk][1]), CORE)
        tall = unpack(sums[chunk][0], crossed, chunk, width, list(tall))
    blocks = [tall[0]] + [send(tall[i], across(*OTHERS[i])) for i in range(1, 8)]

    def block_row(z_at, yh_at, half):
        return (z_at * 2 + yh_at) * (columns // width) + (c + half) % 2 * (columns // width // 2)

    rows_in = [block_row((z + 4 - dz) % 4, (yh + m) % 2, half) for m, dz in OTHERS for half in range(2)]
    rows_out = [block_row((z + dz) % 4, (yh + m) % 2, half) for m, dz in OTHERS for half in range(2)]
    orbit_grad, *leaving = taylor(jnp.stack(rows_in + rows_out).astype(jnp.int32), orbitals, cotangent, blocks)

    arrived = [leaving[0]] + [send(leaving[i], across(*OTHERS[i])) for i in range(1, 8)]
    arrived = [arrived[m * 4 + (4 - dz) % 4] for m, dz in OTHERS]
    gathered, after = [None] * CHUNKS, arrived[0]
    for chunk in PACKED:
        own, crossing = pack(arrived, chunk, after)
        after = own
        rows = jnp.concatenate([own, send(crossing, CORE)], axis=0)
        gathered[chunk] = gather_side_last(rows) if chunk == 0 else gather_side_first(rows)
    field = jnp.zeros((2 * vec_rows, walkers), F32)
    chol_grad = None
    leaving = [None] * CHUNKS
    for chunk in FINISHED:
        given = (at, fields_rel, cholesky, others[chunk])
        if chunk != FINISHED[-1]:
            chol_grad, other, field = finish(*given, field, gathered[chunk], chunk, chol_grad)
        else:
            (field,) = finish(*given, field, gathered[chunk], chunk, None, do_chol=False)
            chol_grad, other = finish(*given, field, gathered[chunk], chunk, chol_grad, do_field=False)
        leaving[chunk] = send(other, CORE)

    natural = lax.dot_general(
        field, order.astype(F32), (((1,), (1,)), ((), ())), precision=lax.Precision.HIGHEST, preferred_element_type=F32
    )
    summed = natural[:vec_rows] + send(natural[vec_rows:].astype(BF16), CORE).astype(F32)
    n_pair = lax.axis_size("pair")
    apart = summed.astype(BF16).reshape(vec_rows, n_pair, walkers // n_pair).transpose(1, 0, 2)
    field_grad = lax.all_to_all(apart, "pair", split_axis=0, concat_axis=0, tiled=True).astype(F32).sum(axis=0)
    chol_grad = place(at, leaving, chol_grad)
    return (orbit_grad, chol_grad, field_grad)


def solution(mesh):
    in_specs = (
        P("walk", "pair"),
        P(),
        P(("pair", "walk"), None, None),
        P(("pair", "walk"), None, None),
    )
    out_specs = (P(("pair", "walk"), None, None), P("walk", "pair"), P("walk", "pair"))

    return jax.shard_map(on_device, mesh=mesh, in_specs=in_specs, out_specs=out_specs, check_vma=False)
```

```python
import functools

import jax
import jax.numpy as jnp
from jax import lax
from jax.experimental import pallas as pl
from jax.experimental.pallas import tpu as pltpu
from jax.sharding import PartitionSpec as P


BF16 = jnp.bfloat16
F32 = jnp.float32
ALL = ("pair", "walk")
CHUNKS = 3
REDUCED = (1, 2, 0)
SUMMED = (1, 0, 2)
PACKED = (1, 0, 2)
FINISHED = (1, 0, 2)
BLOCK = 4096
PLACED = 4
LANES = 128
VMEM = pl.BlockSpec(memory_space=pltpu.VMEM)


def moved(to):
    pairs = []
    for z in range(4):
        for yh in range(2):
            for x in range(4):
                for yl in range(2):
                    for c in range(2):
                        z2, yh2, x2, yl2, c2 = to(z, yh, x, yl, c)
                        here = ((z * 2 + yh) * 4 + x) * 4 + yl * 2 + c
                        there = (((z2 % 4) * 2 + yh2 % 2) * 4 + x2 % 4) * 4 + (yl2 % 2) * 2 + c2 % 2
                        pairs.append((here, there))
    return pairs


CORE = moved(lambda z, yh, x, yl, c: (z, yh, x, yl, c + 1))
SIDE = moved(lambda z, yh, x, yl, c: (z, yh, x, yl + 1, c))
UP = moved(lambda z, yh, x, yl, c: (z, yh, x + 1, yl, c))
DOWN = moved(lambda z, yh, x, yl, c: (z, yh, x + 3, yl, c))
OTHERS = [(m, dz) for m in range(2) for dz in range(4)]


def across(m, dz):
    return moved(lambda z, yh, x, yl, c: (z + dz, yh + m, x, yl + m, c))


def send(array, pairs):
    return lax.ppermute(array, ALL, pairs)


def tied(array, *others):
    return lax.optimization_barrier((array, *others))[0]


def added(*terms):
    total = terms[0].astype(F32)
    for term in terms[1:]:
        total = total + term.astype(F32)
    return total.astype(BF16)


def whole(shape):
    return pl.BlockSpec(shape, lambda *_: (0,) * len(shape))


def take_kernel(start, step, at_ref, all_ref, out_ref, sems):
    column = pl.multiple_of((1 - at_ref[0]) * step + start, LANES)
    copies = []
    for n in range(out_ref.shape[0] // 16):
        rows = slice(16 * n, 16 * n + 16)
        copies.append(
            pltpu.make_async_copy(all_ref.at[rows, pl.ds(column, out_ref.shape[1])], out_ref.at[rows, :], sems.at[n])
        )
    for copy in copies:
        copy.start()
    for copy in copies:
        copy.wait()


def take(at, cholesky, chunk, chunk_width):
    rows = cholesky.shape[0]
    return pl.pallas_call(
        functools.partial(take_kernel, chunk * chunk_width, CHUNKS * chunk_width),
        grid_spec=pltpu.PrefetchScalarGridSpec(
            num_scalar_prefetch=1,
            grid=(1,),
            in_specs=[pl.BlockSpec(memory_space=pl.ANY)],
            out_specs=VMEM,
            scratch_shapes=[pltpu.SemaphoreType.DMA((rows // 16,))],
        ),
        out_shape=jax.ShapeDtypeStruct((rows, chunk_width), BF16),
        name="take",
    )(at, cholesky)


def partial_kernel(groups, at_ref, weights_ref, own_ref, other_ref, after_ref, *outs):
    here = pl.ds(pl.multiple_of(pl.program_id(0) * BLOCK, BLOCK), BLOCK)
    rows = jnp.concatenate([own_ref[...], other_ref[:, here]], axis=0)
    sums = jnp.dot(weights_ref[...], rows, preferred_element_type=F32).astype(BF16)
    for group, out in zip(groups, outs):
        for place, start in enumerate(group):
            out[place * 16 : place * 16 + 16, :] = sums[start : start + 16]


def partial_sums(at, weights, cholesky, other, chunk, groups, after):
    rows, width = other.shape
    steps = width // BLOCK
    return pl.pallas_call(
        functools.partial(partial_kernel, groups),
        grid_spec=pltpu.PrefetchScalarGridSpec(
            num_scalar_prefetch=1,
            grid=(steps,),
            in_specs=[
                whole(weights.shape),
                pl.BlockSpec((rows, BLOCK), lambda i, at: (0, at[0] * (CHUNKS * steps) + chunk * steps + i)),
                VMEM,
                pl.BlockSpec(memory_space=pl.ANY),
            ],
            out_specs=[pl.BlockSpec((16 * len(g), BLOCK), lambda i, at: (0, i)) for g in groups],
        ),
        out_shape=[jax.ShapeDtypeStruct((16 * len(g), width), BF16) for g in groups],
        cost_estimate=pl.CostEstimate(flops=2 * 128 * 128 * width, bytes_accessed=512 * width, transcendentals=0),
        name="partial_sums",
    )(at, weights, cholesky, other, after)


def unpack_kernel(depth, width, n_own, has_outs, *refs):
    own, other = refs[:n_own], refs[n_own : n_own + 1]
    outs, scratch = refs[n_own + 1 + 8 * has_outs : -1], refs[-1]
    across_lanes = width // LANES
    for half, parts in enumerate((own, other)):
        for tile in range(depth * across_lanes):
            lanes = slice(tile * LANES, (tile + 1) * LANES)
            total = parts[0][0:8, lanes].astype(F32)
            for part in parts[1:]:
                total = total + part[0:8, lanes].astype(F32)
            scratch[half, tile * 8 : tile * 8 + 8, :] = total
        for walker in range(8):
            for lane in range(across_lanes):
                tall = [
                    scratch[half, pl.ds((top * across_lanes + lane) * 8 + walker, 8, stride=8 * across_lanes), :]
                    for top in range(0, depth, 8)
                ]
                block = jnp.concatenate(tall, axis=0).astype(BF16)
                outs[walker][half, :, lane * LANES : (lane + 1) * LANES] = block


def unpack(own, other, chunk, width, outs):
    depth = other.shape[1] // width
    arrays = [*own, other]
    specs = [pl.BlockSpec((8, depth * width), lambda i: (0, 0)) for _ in arrays]
    aliases = {}
    if outs:
        aliases = {len(arrays) + n: n for n in range(8)}
        arrays += outs
        specs += [pl.BlockSpec(memory_space=pl.ANY)] * 8
    return pl.pallas_call(
        functools.partial(unpack_kernel, depth, width, len(own), int(bool(outs))),
        grid=(1,),
        in_specs=specs,
        out_specs=[pl.BlockSpec((2, depth, width), lambda i: (0, chunk, 0)) for _ in OTHERS],
        out_shape=[jax.ShapeDtypeStruct((2, CHUNKS * depth, width), BF16) for _ in OTHERS],
        scratch_shapes=[pltpu.VMEM((2, depth * width // LANES * 8, LANES), F32)],
        input_output_aliases=aliases,
        name="unpack",
    )(*arrays)


def pack_kernel(chunk, depth, width, *refs):
    blocks, own, other, scratch = refs[:8], refs[8], refs[9], refs[10]
    across_lanes = width // LANES
    for half, out in enumerate((own, other)):
        for walker in range(8):
            for lane in range(across_lanes):
                tall = blocks[walker][half, chunk * depth : (chunk + 1) * depth, lane * LANES : (lane + 1) * LANES]
                tall = tall.astype(F32)
                for top in range(0, depth, 8):
                    rows = pl.ds((top * across_lanes + lane) * 8 + walker, 8, stride=8 * across_lanes)
                    scratch[half, rows, :] = tall[top : top + 8]
        for tile in range(depth * across_lanes):
            out[:, tile * LANES : (tile + 1) * LANES] = scratch[half, tile * 8 : tile * 8 + 8, :].astype(BF16)


def pack(blocks, chunk, after):
    _, rows, width = blocks[0].shape
    depth = rows // CHUNKS
    return pl.pallas_call(
        lambda *refs: pack_kernel(chunk, depth, width, *refs[:8], *refs[9:]),
        grid=(1,),
        in_specs=[VMEM] * 8 + [pl.BlockSpec(memory_space=pl.ANY)],
        out_specs=[VMEM] * 2,
        out_shape=[jax.ShapeDtypeStruct((8, depth * width), BF16)] * 2,
        scratch_shapes=[pltpu.VMEM((2, depth * width // LANES * 8, LANES), F32)],
        name="pack",
    )(*blocks, after)


def taylor_kernel(n_blocks, depths, at_ref, orbit_ref, cotan_ref, *refs):
    blocks, orbit_out, outs = refs[:n_blocks], refs[n_blocks], refs[n_blocks + 1 : 2 * n_blocks + 1]
    matrix, grad, series, adjoint = refs[2 * n_blocks + 1 :]
    width = matrix.shape[0]
    tile = 256
    for n, block in enumerate(blocks):
        for half in range(2):
            row = pl.multiple_of(at_ref[2 * n + half], 16)
            matrix[pl.ds(row, depths[n]), :] = block[half]
    series[0] = orbit_ref[0]
    adjoint[4] = cotan_ref[0]

    def tiles(body):
        def step(i, carry):
            body(pl.ds(pl.multiple_of(i * tile, tile), tile))
            return carry

        lax.fori_loop(0, width // tile, step, 0)

    for degree in (1, 2, 3):
        down = 4 - degree

        def both(at, degree=degree, down=down):
            product = lax.dot_general(
                series[degree - 1], matrix[at, :], (((1,), (1,)), ((), ())), preferred_element_type=F32
            )
            series[degree, :, at] = (product / degree).astype(BF16)
            product = jnp.dot(adjoint[down + 1], matrix[:, at], preferred_element_type=F32)
            adjoint[down, :, at] = (cotan_ref[0, :, at].astype(F32) + product / (down + 1)).astype(BF16)

        tiles(both)

    def last(at):
        product = jnp.dot(adjoint[1], matrix[:, at], preferred_element_type=F32)
        orbit_out[0, :, at] = (cotan_ref[0, :, at].astype(F32) + product).astype(BF16)
        total = None
        for degree in range(1, 5):
            term = lax.dot_general(
                adjoint[degree, :, at], series[degree - 1], (((0,), (0,)), ((), ())), preferred_element_type=F32
            )
            total = term if total is None else total + term / degree
        grad[at, :] = total.astype(BF16)

    tiles(last)
    for n, out in enumerate(outs):
        for half in range(2):
            row = pl.multiple_of(at_ref[2 * n_blocks + 2 * n + half], 16)
            out[half] = grad[pl.ds(row, depths[n]), :]


def taylor(at, orbitals, cotangent, blocks):
    width = orbitals.shape[2]
    n = len(blocks)
    specs = [VMEM] * n
    return pl.pallas_call(
        functools.partial(taylor_kernel, n, [block.shape[1] for block in blocks]),
        grid_spec=pltpu.PrefetchScalarGridSpec(
            num_scalar_prefetch=1,
            grid=(1,),
            in_specs=[VMEM, VMEM] + specs,
            out_specs=[VMEM] + specs,
            scratch_shapes=[
                pltpu.VMEM((width, width), BF16),
                pltpu.VMEM((width, width), BF16),
                pltpu.VMEM((4, orbitals.shape[1], width), BF16),
                pltpu.VMEM((5, orbitals.shape[1], width), BF16),
            ],
        ),
        out_shape=[jax.ShapeDtypeStruct(orbitals.shape, BF16)]
        + [jax.ShapeDtypeStruct(block.shape, BF16) for block in blocks],
        name="taylor",
    )(at, orbitals, cotangent, *blocks)


def field_kernel(n_parts, own_ref, other_ref, field_ref, *refs):
    grads = jnp.concatenate([part[...] for part in refs[:n_parts]], axis=0)
    rows = jnp.concatenate([own_ref[...], other_ref[...]], axis=0)
    refs[-1][...] += lax.dot_general(rows, grads, (((1,), (1,)), ((), ())), preferred_element_type=F32)


def chol_kernel(n_parts, weights_ref, *refs):
    grads = jnp.concatenate([part[...] for part in refs[:n_parts]], axis=0)
    total = jnp.dot(weights_ref[...], grads, preferred_element_type=F32).astype(BF16)
    chol_out, other_out = refs[-2:]
    half = total.shape[0] // 2
    chol_out[...] = total[:half]
    other_out[...] = total[half:]


def finish_kernel(n_parts, has_out, do_field, do_chol, at_ref, *refs):
    refs = list(refs)
    weights = [refs.pop(0)] if do_chol else []
    columns = [refs.pop(0) for _ in range(3)] if do_field else []
    parts, refs = refs[:n_parts], refs[n_parts + has_out :]
    if do_field:

        @pl.when(pl.program_id(0) == 0)
        def _():
            refs[-1][...] = columns[2][...]

        field_kernel(n_parts, *columns, *parts, refs[-1])
    if do_chol:
        chol_kernel(n_parts, *weights, *parts, *refs[:2])


def finish(at, weights, cholesky, other, field, parts, chunk, out, do_field=True, do_chol=True):
    rows, width = other.shape
    steps = width // BLOCK
    here = pl.BlockSpec((rows, BLOCK), lambda i, at: (0, at[0] * (CHUNKS * steps) + chunk * steps + i))
    along = pl.BlockSpec((rows, BLOCK), lambda i, at: (0, i))
    args, in_specs, out_specs, out_shape, aliases = [at], [], [], [], {}
    if do_chol:
        args.append(weights)
        in_specs.append(whole(weights.shape))
        out_specs += [here, along]
        out_shape += [jax.ShapeDtypeStruct(cholesky.shape, BF16), jax.ShapeDtypeStruct((rows, width), BF16)]
    if do_field:
        args += [cholesky, other, field]
        in_specs += [here, along, whole(field.shape)]
        out_specs.append(whole(field.shape))
        out_shape.append(jax.ShapeDtypeStruct(field.shape, F32))
    for part in parts:
        array, row = part if isinstance(part, tuple) else (part, None)
        height = array.shape[0] if row is None else 16
        args.append(array)
        in_specs.append(pl.BlockSpec((height, BLOCK), lambda i, at, row=row or 0: (row, i)))
    if do_chol and out is not None:
        aliases = {len(args): 0}
        args.append(out)
        in_specs.append(pl.BlockSpec(memory_space=pl.ANY))
    return pl.pallas_call(
        functools.partial(finish_kernel, len(parts), len(aliases), do_field, do_chol),
        grid_spec=pltpu.PrefetchScalarGridSpec(
            num_scalar_prefetch=1, grid=(steps,), in_specs=in_specs, out_specs=out_specs
        ),
        out_shape=out_shape,
        input_output_aliases=aliases,
        cost_estimate=pl.CostEstimate(flops=4 * 128 * 128 * width, bytes_accessed=768 * width, transcendentals=0),
        name="finish",
    )(*args)


def place_kernel(starts, step, at_ref, *refs):
    pieces, out_ref, sems = refs[: len(starts)], refs[len(starts) + 1], refs[len(starts) + 2]
    copies = []
    for n, (piece, start) in enumerate(zip(pieces, starts)):
        column = pl.multiple_of((1 - at_ref[0]) * step + start, LANES)
        for m in range(PLACED):
            rows = slice(m * piece.shape[0] // PLACED, (m + 1) * piece.shape[0] // PLACED)
            copies.append(
                pltpu.make_async_copy(
                    piece.at[rows, :], out_ref.at[rows, pl.ds(column, piece.shape[1])], sems.at[n * PLACED + m]
                )
            )
    for copy in copies:
        copy.start()
    for copy in copies:
        copy.wait()


def place(at, pieces, chunks, out):
    width = pieces[0].shape[1]
    n = len(pieces)
    return pl.pallas_call(
        functools.partial(place_kernel, [chunk * width for chunk in chunks], CHUNKS * width),
        grid_spec=pltpu.PrefetchScalarGridSpec(
            num_scalar_prefetch=1,
            grid=(1,),
            in_specs=[VMEM] * n + [pl.BlockSpec(memory_space=pl.ANY)],
            out_specs=pl.BlockSpec(memory_space=pl.ANY),
            scratch_shapes=[pltpu.SemaphoreType.DMA((n * PLACED,))],
        ),
        out_shape=jax.ShapeDtypeStruct(out.shape, out.dtype),
        input_output_aliases={n + 1: 0},
        name="place",
    )(at, *pieces, out)


def reduce_side_last(parts, tie):
    far_up, far_down, near_up, free_up, free_down, near_down, here0, here1 = parts
    up, down = send(far_up, UP), send(far_down, DOWN)
    free_up, free_down = send(free_up, UP), send(free_down, DOWN)
    up, down = added(near_up, up), added(near_down, down)
    up, down = send(up, UP), send(down, DOWN)
    side = send(added(tied(here1, tie), free_up, down), SIDE)
    return [here0, up, free_down, side], [t[8:16] for t in (here0, up, free_down, side)]


def reduce_side_first(parts):
    leaving, staying = parts
    side = send(leaving, SIDE)

    def row(dx, half):
        rows = slice(dx * 16 + half * 8, dx * 16 + half * 8 + 8)
        return staying[rows], side[rows]

    far_up, far_down = lax.optimization_barrier((added(*row(2, 0)), added(*row(2, 1))))
    up, down = send(far_up, UP), send(far_down, DOWN)
    near_up = jnp.concatenate([added(*row(1, 0), up), added(*row(1, 1))], axis=0)
    near_down = jnp.concatenate([added(*row(3, 0)), added(*row(3, 1), down)], axis=0)
    up, down = send(near_up, UP), send(near_down, DOWN)
    return [staying, side, up, down], [t[8:16] for t in (staying, side, up, down)], (far_down, near_down)


def gather_side_first(rows):
    rows = jnp.concatenate([rows, send(rows, SIDE)], axis=0)
    low, high = send(rows, UP), send(rows, DOWN)
    far0, far1 = low[:16], high[16:]
    far0, far1 = send(far0, UP), send(far1, DOWN)
    return [rows, high, far0, far1, low]


def gather_side_last(rows):
    low, high = send(rows, UP), send(rows, DOWN)
    far0, far1 = send(low[:8], UP), send(high[8:], DOWN)
    rows_s = send(rows, SIDE)
    near_s = send(jnp.concatenate([high, low], axis=0), SIDE)
    far_s = send(jnp.concatenate([far0, far1], axis=0), SIDE)
    return [rows, rows_s, (high, 0), (near_s, 0), far0, far1, far_s, (low, 0), (near_s, 1)]


SIDE_LAST_GROUPS = ((64,), (80,), (32,), (48,), (96,), (112,), (0,), (16,))
SIDE_FIRST_GROUPS = ((16, 48, 80, 112), (0, 32, 64, 96))


def summed_of(at, weights, cholesky, others, chunk, after):
    groups = SIDE_FIRST_GROUPS if chunk == 0 else SIDE_LAST_GROUPS
    return partial_sums(at, weights, cholesky, others[chunk], chunk, groups, after)


def on_device(cholesky, fields, orbitals, cotangent):
    vec_rows, columns = cholesky.shape
    walkers = fields.shape[1]
    width = orbitals.shape[2]
    chunk_width = columns // (2 * CHUNKS)
    pair, walk = lax.axis_index("pair"), lax.axis_index("walk")
    z, yh = pair // 2, pair % 2
    x, yl, c = walk // 4, (walk // 2) % 2, walk % 2
    at = jnp.reshape(c, (1,)).astype(jnp.int32)

    r = lax.broadcasted_iota(jnp.int32, (walkers, walkers), 1)
    dx, dyl, dc, m, dz = r // 32, (r // 16) % 2, (r // 8) % 2, (r // 4) % 2, r % 4
    walker_z, walker_yh = (z + dz) % 4, (yh + m) % 2
    walker_x, walker_yl, walker_c = (x + dx) % 4, (yl + dyl + m) % 2, (c + dc) % 2
    walker = (walker_z * 2 + walker_yh) * 16 + walker_x * 4 + walker_yl * 2 + walker_c
    order = lax.broadcasted_iota(jnp.int32, (walkers, walkers), 0) == walker
    fields_here = jnp.concatenate(
        [
            lax.dynamic_slice_in_dim(fields, walk * vec_rows, vec_rows, 0),
            lax.dynamic_slice_in_dim(fields, (walk + 1 - 2 * c) * vec_rows, vec_rows, 0),
        ],
        axis=0,
    )
    fields_rel = jnp.dot(fields_here, order.astype(BF16), preferred_element_type=F32).astype(BF16)
    fields_turned = lax.dot_general(
        order.astype(BF16), fields_here, (((0,), (1,)), ((), ())), preferred_element_type=F32
    ).astype(BF16)

    others, sums, after, ties = [None] * CHUNKS, [None] * CHUNKS, fields_turned, None
    partials = [None] * CHUNKS
    for place_at, chunk in enumerate(SUMMED):
        whole_rows = cholesky if place_at < 2 else tied(cholesky, partials[SUMMED[0]][0])
        leaving = take(at, whole_rows, chunk, chunk_width)
        others[chunk] = send(leaving, CORE)
        if place_at == 1:
            partials[SUMMED[0]] = summed_of(at, fields_turned, cholesky, others, SUMMED[0], fields_turned)
    for last, chunk in zip(SUMMED, SUMMED[1:]):
        partials[chunk] = summed_of(at, fields_turned, cholesky, others, chunk, partials[last][0])
    *sums[0], ties = reduce_side_first(partials[0])
    for chunk in (1, 2):
        sums[chunk] = reduce_side_last(partials[chunk], ties[chunk - 1])
    tall = []
    for chunk in REDUCED:
        crossed = send(added(*sums[chunk][1]), CORE)
        tall = unpack(sums[chunk][0], crossed, chunk, width, list(tall))
    blocks = [tall[0]] + [send(tall[i], across(*OTHERS[i])) for i in range(1, 8)]

    def block_row(z_at, yh_at, half):
        return (z_at * 2 + yh_at) * (columns // width) + (c + half) % 2 * (columns // width // 2)

    rows_in = [block_row((z + 4 - dz) % 4, (yh + m) % 2, half) for m, dz in OTHERS for half in range(2)]
    rows_out = [block_row((z + dz) % 4, (yh + m) % 2, half) for m, dz in OTHERS for half in range(2)]
    orbit_grad, *leaving = taylor(jnp.stack(rows_in + rows_out).astype(jnp.int32), orbitals, cotangent, blocks)

    arrived = [leaving[0]] + [send(leaving[i], across(*OTHERS[i])) for i in range(1, 8)]
    arrived = [arrived[m * 4 + (4 - dz) % 4] for m, dz in OTHERS]
    gathered, after = [None] * CHUNKS, arrived[0]
    for chunk in PACKED:
        own, crossing = pack(arrived, chunk, after)
        after = own
        rows = jnp.concatenate([own, send(crossing, CORE)], axis=0)
        gathered[chunk] = gather_side_last(rows) if chunk == 0 else gather_side_first(rows)
    field = jnp.zeros((2 * vec_rows, walkers), F32)
    chol_grad = None
    leaving = []
    for chunk in FINISHED:
        given = (at, fields_rel, cholesky, others[chunk])
        if chunk == FINISHED[-1]:
            chol_grad = place(at, leaving, FINISHED[:-1], chol_grad)
            leaving = []
        if chunk != FINISHED[-1]:
            chol_grad, other, field = finish(*given, field, gathered[chunk], chunk, chol_grad)
        else:
            (field,) = finish(*given, field, gathered[chunk], chunk, None, do_chol=False)
            chol_grad, other = finish(*given, field, gathered[chunk], chunk, chol_grad, do_field=False)
        leaving.append(send(other, CORE))

    natural = lax.dot_general(
        field, order.astype(F32), (((1,), (1,)), ((), ())), precision=lax.Precision.HIGHEST, preferred_element_type=F32
    )
    summed = natural[:vec_rows] + send(natural[vec_rows:].astype(BF16), CORE).astype(F32)
    n_pair = lax.axis_size("pair")
    apart = summed.astype(BF16).reshape(vec_rows, n_pair, walkers // n_pair).transpose(1, 0, 2)
    field_grad = lax.all_to_all(apart, "pair", split_axis=0, concat_axis=0, tiled=True).astype(F32).sum(axis=0)
    chol_grad = place(at, leaving, FINISHED[-1:], chol_grad)
    return (orbit_grad, chol_grad, field_grad)


def solution(mesh):
    in_specs = (
        P("walk", "pair"),
        P(),
        P(("pair", "walk"), None, None),
        P(("pair", "walk"), None, None),
    )
    out_specs = (P(("pair", "walk"), None, None), P("walk", "pair"), P("walk", "pair"))

    return jax.shard_map(on_device, mesh=mesh, in_specs=in_specs, out_specs=out_specs, check_vma=False)
```

```python
import functools

import jax
import jax.numpy as jnp
from jax import lax
from jax.experimental import pallas as pl
from jax.experimental.pallas import tpu as pltpu
from jax.sharding import PartitionSpec as P


BF16 = jnp.bfloat16
F32 = jnp.float32
ALL = ("pair", "walk")
CHUNKS = 3
REDUCED = (1, 2, 0)
SUMMED = (1, 0, 2)
PACKED = (1, 0, 2)
FINISHED = (1, 0, 2)
BLOCK = 4096
PLACED = 4
LANES = 128
VMEM = pl.BlockSpec(memory_space=pltpu.VMEM)


def moved(to):
    pairs = []
    for z in range(4):
        for yh in range(2):
            for x in range(4):
                for yl in range(2):
                    for c in range(2):
                        z2, yh2, x2, yl2, c2 = to(z, yh, x, yl, c)
                        here = ((z * 2 + yh) * 4 + x) * 4 + yl * 2 + c
                        there = (((z2 % 4) * 2 + yh2 % 2) * 4 + x2 % 4) * 4 + (yl2 % 2) * 2 + c2 % 2
                        pairs.append((here, there))
    return pairs


CORE = moved(lambda z, yh, x, yl, c: (z, yh, x, yl, c + 1))
SIDE = moved(lambda z, yh, x, yl, c: (z, yh, x, yl + 1, c))
UP = moved(lambda z, yh, x, yl, c: (z, yh, x + 1, yl, c))
DOWN = moved(lambda z, yh, x, yl, c: (z, yh, x + 3, yl, c))
OTHERS = [(m, dz) for m in range(2) for dz in range(4)]


def across(m, dz):
    return moved(lambda z, yh, x, yl, c: (z + dz, yh + m, x, yl + m, c))


def send(array, pairs):
    return lax.ppermute(array, ALL, pairs)


def tied(array, *others):
    return lax.optimization_barrier((array, *others))[0]


def added(*terms):
    total = terms[0].astype(F32)
    for term in terms[1:]:
        total = total + term.astype(F32)
    return total.astype(BF16)


def whole(shape):
    return pl.BlockSpec(shape, lambda *_: (0,) * len(shape))


def take_kernel(start, step, at_ref, all_ref, out_ref, sems):
    column = pl.multiple_of((1 - at_ref[0]) * step + start, LANES)
    copies = []
    for n in range(out_ref.shape[0] // 16):
        rows = slice(16 * n, 16 * n + 16)
        copies.append(
            pltpu.make_async_copy(all_ref.at[rows, pl.ds(column, out_ref.shape[1])], out_ref.at[rows, :], sems.at[n])
        )
    for copy in copies:
        copy.start()
    for copy in copies:
        copy.wait()


def take(at, cholesky, chunk, chunk_width):
    rows = cholesky.shape[0]
    return pl.pallas_call(
        functools.partial(take_kernel, chunk * chunk_width, CHUNKS * chunk_width),
        grid_spec=pltpu.PrefetchScalarGridSpec(
            num_scalar_prefetch=1,
            grid=(1,),
            in_specs=[pl.BlockSpec(memory_space=pl.ANY)],
            out_specs=VMEM,
            scratch_shapes=[pltpu.SemaphoreType.DMA((rows // 16,))],
        ),
        out_shape=jax.ShapeDtypeStruct((rows, chunk_width), BF16),
        name="take",
    )(at, cholesky)


def partial_kernel(groups, at_ref, weights_ref, own_ref, other_ref, after_ref, *outs):
    here = pl.ds(pl.multiple_of(pl.program_id(0) * BLOCK, BLOCK), BLOCK)
    rows = jnp.concatenate([own_ref[...], other_ref[:, here]], axis=0)
    sums = jnp.dot(weights_ref[...], rows, preferred_element_type=F32).astype(BF16)
    for group, out in zip(groups, outs):
        for place, start in enumerate(group):
            out[place * 16 : place * 16 + 16, :] = sums[start : start + 16]


def partial_sums(at, weights, cholesky, other, chunk, groups, after):
    rows, width = other.shape
    steps = width // BLOCK
    return pl.pallas_call(
        functools.partial(partial_kernel, groups),
        grid_spec=pltpu.PrefetchScalarGridSpec(
            num_scalar_prefetch=1,
            grid=(steps,),
            in_specs=[
                whole(weights.shape),
                pl.BlockSpec((rows, BLOCK), lambda i, at: (0, at[0] * (CHUNKS * steps) + chunk * steps + i)),
                VMEM,
                pl.BlockSpec(memory_space=pl.ANY),
            ],
            out_specs=[pl.BlockSpec((16 * len(g), BLOCK), lambda i, at: (0, i)) for g in groups],
        ),
        out_shape=[jax.ShapeDtypeStruct((16 * len(g), width), BF16) for g in groups],
        cost_estimate=pl.CostEstimate(flops=2 * 128 * 128 * width, bytes_accessed=512 * width, transcendentals=0),
        name="partial_sums",
    )(at, weights, cholesky, other, after)


def unpack_kernel(depth, width, n_own, has_outs, *refs):
    own, other = refs[:n_own], refs[n_own : n_own + 1]
    outs, scratch = refs[n_own + 1 + 8 * has_outs : -1], refs[-1]
    across_lanes = width // LANES
    for half, parts in enumerate((own, other)):
        for tile in range(depth * across_lanes):
            lanes = slice(tile * LANES, (tile + 1) * LANES)
            total = parts[0][0:8, lanes].astype(F32)
            for part in parts[1:]:
                total = total + part[0:8, lanes].astype(F32)
            scratch[half, tile * 8 : tile * 8 + 8, :] = total
        for walker in range(8):
            for lane in range(across_lanes):
                tall = [
                    scratch[half, pl.ds((top * across_lanes + lane) * 8 + walker, 8, stride=8 * across_lanes), :]
                    for top in range(0, depth, 8)
                ]
                block = jnp.concatenate(tall, axis=0).astype(BF16)
                outs[walker][half, :, lane * LANES : (lane + 1) * LANES] = block


def unpack(own, other, chunk, width, outs):
    depth = other.shape[1] // width
    arrays = [*own, other]
    specs = [pl.BlockSpec((8, depth * width), lambda i: (0, 0)) for _ in own] + [VMEM]
    aliases = {}
    if outs:
        aliases = {len(arrays) + n: n for n in range(8)}
        arrays += outs
        specs += [pl.BlockSpec(memory_space=pl.ANY)] * 8
    return pl.pallas_call(
        functools.partial(unpack_kernel, depth, width, len(own), int(bool(outs))),
        grid=(1,),
        in_specs=specs,
        out_specs=[pl.BlockSpec((2, depth, width), lambda i: (0, chunk, 0)) for _ in OTHERS],
        out_shape=[jax.ShapeDtypeStruct((2, CHUNKS * depth, width), BF16) for _ in OTHERS],
        scratch_shapes=[pltpu.VMEM((2, depth * width // LANES * 8, LANES), F32)],
        input_output_aliases=aliases,
        name="unpack",
    )(*arrays)


def pack_kernel(depth, width, *refs):
    blocks, own, other, scratch = refs[:8], refs[8], refs[9], refs[10]
    across_lanes = width // LANES
    for half, out in enumerate((own, other)):
        for walker in range(8):
            for lane in range(across_lanes):
                tall = blocks[walker][half, :, lane * LANES : (lane + 1) * LANES].astype(F32)
                for top in range(0, depth, 8):
                    rows = pl.ds((top * across_lanes + lane) * 8 + walker, 8, stride=8 * across_lanes)
                    scratch[half, rows, :] = tall[top : top + 8]
        for tile in range(depth * across_lanes):
            out[:, tile * LANES : (tile + 1) * LANES] = scratch[half, tile * 8 : tile * 8 + 8, :].astype(BF16)


def pack(blocks, chunk, after):
    _, rows, width = blocks[0].shape
    depth = rows // CHUNKS
    return pl.pallas_call(
        lambda *refs: pack_kernel(depth, width, *refs[:8], *refs[9:]),
        grid=(1,),
        in_specs=[pl.BlockSpec((2, depth, width), lambda i: (0, chunk, 0)) for _ in blocks]
        + [pl.BlockSpec(memory_space=pl.ANY)],
        out_specs=[VMEM] * 2,
        out_shape=[jax.ShapeDtypeStruct((8, depth * width), BF16)] * 2,
        scratch_shapes=[pltpu.VMEM((2, depth * width // LANES * 8, LANES), F32)],
        name="pack",
    )(*blocks, after)


def taylor_kernel(n_blocks, depths, at_ref, orbit_ref, cotan_ref, *refs):
    blocks, orbit_out, outs = refs[:n_blocks], refs[n_blocks], refs[n_blocks + 1 : 2 * n_blocks + 1]
    matrix, grad, series, adjoint = refs[2 * n_blocks + 1 :]
    width = matrix.shape[0]
    tile = 256
    for n, block in enumerate(blocks):
        for half in range(2):
            row = pl.multiple_of(at_ref[2 * n + half], 16)
            matrix[pl.ds(row, depths[n]), :] = block[half]
    series[0] = orbit_ref[0]
    adjoint[4] = cotan_ref[0]

    def tiles(body):
        for start in range(0, width, tile):
            body(slice(start, start + tile))

    for degree in (1, 2, 3):
        down = 4 - degree

        def both(at, degree=degree, down=down):
            product = lax.dot_general(
                series[degree - 1], matrix[at, :], (((1,), (1,)), ((), ())), preferred_element_type=F32
            )
            series[degree, :, at] = (product / degree).astype(BF16)
            product = jnp.dot(adjoint[down + 1], matrix[:, at], preferred_element_type=F32)
            adjoint[down, :, at] = (cotan_ref[0, :, at].astype(F32) + product / (down + 1)).astype(BF16)

        tiles(both)

    def last(at):
        product = jnp.dot(adjoint[1], matrix[:, at], preferred_element_type=F32)
        orbit_out[0, :, at] = (cotan_ref[0, :, at].astype(F32) + product).astype(BF16)
        total = None
        for degree in range(1, 5):
            term = lax.dot_general(
                adjoint[degree, :, at], series[degree - 1], (((0,), (0,)), ((), ())), preferred_element_type=F32
            )
            total = term if total is None else total + term / degree
        grad[at, :] = total.astype(BF16)

    tiles(last)
    for n, out in enumerate(outs):
        for half in range(2):
            row = pl.multiple_of(at_ref[2 * n_blocks + 2 * n + half], 16)
            out[half] = grad[pl.ds(row, depths[n]), :]


def taylor(at, orbitals, cotangent, blocks):
    width = orbitals.shape[2]
    n = len(blocks)
    specs = [VMEM] * n
    return pl.pallas_call(
        functools.partial(taylor_kernel, n, [block.shape[1] for block in blocks]),
        grid_spec=pltpu.PrefetchScalarGridSpec(
            num_scalar_prefetch=1,
            grid=(1,),
            in_specs=[VMEM, VMEM] + specs,
            out_specs=[VMEM] + specs,
            scratch_shapes=[
                pltpu.VMEM((width, width), BF16),
                pltpu.VMEM((width, width), BF16),
                pltpu.VMEM((4, orbitals.shape[1], width), BF16),
                pltpu.VMEM((5, orbitals.shape[1], width), BF16),
            ],
        ),
        out_shape=[jax.ShapeDtypeStruct(orbitals.shape, BF16)]
        + [jax.ShapeDtypeStruct(block.shape, BF16) for block in blocks],
        name="taylor",
    )(at, orbitals, cotangent, *blocks)


def field_kernel(n_parts, own_ref, other_ref, field_ref, *refs):
    grads = jnp.concatenate([part[...] for part in refs[:n_parts]], axis=0)
    rows = jnp.concatenate([own_ref[...], other_ref[...]], axis=0)
    refs[-1][...] += lax.dot_general(rows, grads, (((1,), (1,)), ((), ())), preferred_element_type=F32)


def chol_kernel(n_parts, weights_ref, *refs):
    grads = jnp.concatenate([part[...] for part in refs[:n_parts]], axis=0)
    total = jnp.dot(weights_ref[...], grads, preferred_element_type=F32).astype(BF16)
    chol_out, other_out = refs[-2:]
    half = total.shape[0] // 2
    chol_out[...] = total[:half]
    other_out[...] = total[half:]


def finish_kernel(n_parts, has_out, do_field, do_chol, at_ref, *refs):
    refs = list(refs)
    weights = [refs.pop(0)] if do_chol else []
    columns = [refs.pop(0) for _ in range(3)] if do_field else []
    parts, refs = refs[:n_parts], refs[n_parts + has_out :]
    if do_field:

        @pl.when(pl.program_id(0) == 0)
        def _():
            refs[-1][...] = columns[2][...]

        field_kernel(n_parts, *columns, *parts, refs[-1])
    if do_chol:
        chol_kernel(n_parts, *weights, *parts, *refs[:2])


def finish(at, weights, cholesky, other, field, parts, chunk, out, do_field=True, do_chol=True):
    rows, width = other.shape
    steps = width // BLOCK
    here = pl.BlockSpec((rows, BLOCK), lambda i, at: (0, at[0] * (CHUNKS * steps) + chunk * steps + i))
    along = pl.BlockSpec((rows, BLOCK), lambda i, at: (0, i))
    args, in_specs, out_specs, out_shape, aliases = [at], [], [], [], {}
    if do_chol:
        args.append(weights)
        in_specs.append(whole(weights.shape))
        out_specs += [here, along]
        out_shape += [jax.ShapeDtypeStruct(cholesky.shape, BF16), jax.ShapeDtypeStruct((rows, width), BF16)]
    if do_field:
        args += [cholesky, other, field]
        in_specs += [here, along, whole(field.shape)]
        out_specs.append(whole(field.shape))
        out_shape.append(jax.ShapeDtypeStruct(field.shape, F32))
    for part in parts:
        array, row = part if isinstance(part, tuple) else (part, None)
        height = array.shape[0] if row is None else 16
        args.append(array)
        in_specs.append(pl.BlockSpec((height, BLOCK), lambda i, at, row=row or 0: (row, i)))
    if do_chol and out is not None:
        aliases = {len(args): 0}
        args.append(out)
        in_specs.append(pl.BlockSpec(memory_space=pl.ANY))
    return pl.pallas_call(
        functools.partial(finish_kernel, len(parts), len(aliases), do_field, do_chol),
        grid_spec=pltpu.PrefetchScalarGridSpec(
            num_scalar_prefetch=1, grid=(steps,), in_specs=in_specs, out_specs=out_specs
        ),
        out_shape=out_shape,
        input_output_aliases=aliases,
        cost_estimate=pl.CostEstimate(flops=4 * 128 * 128 * width, bytes_accessed=768 * width, transcendentals=0),
        name="finish",
    )(*args)


def place_kernel(starts, step, at_ref, *refs):
    pieces, out_ref, sems = refs[: len(starts)], refs[len(starts) + 1], refs[len(starts) + 2]
    copies = []
    for n, (piece, start) in enumerate(zip(pieces, starts)):
        column = pl.multiple_of((1 - at_ref[0]) * step + start, LANES)
        for m in range(PLACED):
            rows = slice(m * piece.shape[0] // PLACED, (m + 1) * piece.shape[0] // PLACED)
            copies.append(
                pltpu.make_async_copy(
                    piece.at[rows, :], out_ref.at[rows, pl.ds(column, piece.shape[1])], sems.at[n * PLACED + m]
                )
            )
    for copy in copies:
        copy.start()
    for copy in copies:
        copy.wait()


def place(at, pieces, chunks, out):
    width = pieces[0].shape[1]
    n = len(pieces)
    return pl.pallas_call(
        functools.partial(place_kernel, [chunk * width for chunk in chunks], CHUNKS * width),
        grid_spec=pltpu.PrefetchScalarGridSpec(
            num_scalar_prefetch=1,
            grid=(1,),
            in_specs=[VMEM] * n + [pl.BlockSpec(memory_space=pl.ANY)],
            out_specs=pl.BlockSpec(memory_space=pl.ANY),
            scratch_shapes=[pltpu.SemaphoreType.DMA((n * PLACED,))],
        ),
        out_shape=jax.ShapeDtypeStruct(out.shape, out.dtype),
        input_output_aliases={n + 1: 0},
        name="place",
    )(at, *pieces, out)


def reduce_side_last(parts, tie):
    far_up, far_down, near_up, free_up, free_down, near_down, here0, here1 = parts
    up, down = send(far_up, UP), send(far_down, DOWN)
    free_up, free_down = send(free_up, UP), send(free_down, DOWN)
    up, down = added(near_up, up), added(near_down, down)
    up, down = send(up, UP), send(down, DOWN)
    side = send(added(tied(here1, tie), free_up, down), SIDE)
    return [here0, up, free_down, side], [t[8:16] for t in (here0, up, free_down, side)]


def reduce_side_first(parts):
    leaving, staying = parts
    side = send(leaving, SIDE)

    def row(dx, half):
        rows = slice(dx * 16 + half * 8, dx * 16 + half * 8 + 8)
        return staying[rows], side[rows]

    far_up, far_down = lax.optimization_barrier((added(*row(2, 0)), added(*row(2, 1))))
    up, down = send(far_up, UP), send(far_down, DOWN)
    near_up = jnp.concatenate([added(*row(1, 0), up), added(*row(1, 1))], axis=0)
    near_down = jnp.concatenate([added(*row(3, 0)), added(*row(3, 1), down)], axis=0)
    up, down = send(near_up, UP), send(near_down, DOWN)
    return [staying, side, up, down], [t[8:16] for t in (staying, side, up, down)], (far_down, near_down)


def gather_side_first(rows):
    rows = jnp.concatenate([rows, send(rows, SIDE)], axis=0)
    low, high = send(rows, UP), send(rows, DOWN)
    far0, far1 = low[:16], high[16:]
    far0, far1 = send(far0, UP), send(far1, DOWN)
    return [rows, high, far0, far1, low]


def gather_side_last(rows):
    low, high = send(rows, UP), send(rows, DOWN)
    far0, far1 = send(low[:8], UP), send(high[8:], DOWN)
    rows_s = send(rows, SIDE)
    near_s = send(jnp.concatenate([high, low], axis=0), SIDE)
    far_s = send(jnp.concatenate([far0, far1], axis=0), SIDE)
    return [rows, rows_s, (high, 0), (near_s, 0), far0, far1, far_s, (low, 0), (near_s, 1)]


SIDE_LAST_GROUPS = ((64,), (80,), (32,), (48,), (96,), (112,), (0,), (16,))
SIDE_FIRST_GROUPS = ((16, 48, 80, 112), (0, 32, 64, 96))


def summed_of(at, weights, cholesky, others, chunk, after):
    groups = SIDE_FIRST_GROUPS if chunk == 0 else SIDE_LAST_GROUPS
    return partial_sums(at, weights, cholesky, others[chunk], chunk, groups, after)


def on_device(cholesky, fields, orbitals, cotangent):
    vec_rows, columns = cholesky.shape
    walkers = fields.shape[1]
    width = orbitals.shape[2]
    chunk_width = columns // (2 * CHUNKS)
    pair, walk = lax.axis_index("pair"), lax.axis_index("walk")
    z, yh = pair // 2, pair % 2
    x, yl, c = walk // 4, (walk // 2) % 2, walk % 2
    at = jnp.reshape(c, (1,)).astype(jnp.int32)

    r = lax.broadcasted_iota(jnp.int32, (walkers, walkers), 1)
    dx, dyl, dc, m, dz = r // 32, (r // 16) % 2, (r // 8) % 2, (r // 4) % 2, r % 4
    walker_z, walker_yh = (z + dz) % 4, (yh + m) % 2
    walker_x, walker_yl, walker_c = (x + dx) % 4, (yl + dyl + m) % 2, (c + dc) % 2
    walker = (walker_z * 2 + walker_yh) * 16 + walker_x * 4 + walker_yl * 2 + walker_c
    order = lax.broadcasted_iota(jnp.int32, (walkers, walkers), 0) == walker
    fields_here = jnp.concatenate(
        [
            lax.dynamic_slice_in_dim(fields, walk * vec_rows, vec_rows, 0),
            lax.dynamic_slice_in_dim(fields, (walk + 1 - 2 * c) * vec_rows, vec_rows, 0),
        ],
        axis=0,
    )
    fields_rel = jnp.dot(fields_here, order.astype(BF16), preferred_element_type=F32).astype(BF16)
    fields_turned = lax.dot_general(
        order.astype(BF16), fields_here, (((0,), (1,)), ((), ())), preferred_element_type=F32
    ).astype(BF16)

    others, sums, after, ties = [None] * CHUNKS, [None] * CHUNKS, fields_turned, None
    partials = [None] * CHUNKS
    for place_at, chunk in enumerate(SUMMED):
        whole_rows = cholesky if place_at < 2 else tied(cholesky, partials[SUMMED[0]][0])
        leaving = take(at, whole_rows, chunk, chunk_width)
        others[chunk] = send(leaving, CORE)
        if place_at == 1:
            partials[SUMMED[0]] = summed_of(at, fields_turned, cholesky, others, SUMMED[0], fields_turned)
    for last, chunk in zip(SUMMED, SUMMED[1:]):
        partials[chunk] = summed_of(at, fields_turned, cholesky, others, chunk, partials[last][0])
    *sums[0], ties = reduce_side_first(partials[0])
    for chunk in (1, 2):
        sums[chunk] = reduce_side_last(partials[chunk], ties[chunk - 1])
    tall = []
    for chunk in REDUCED:
        crossed = send(added(*sums[chunk][1]), CORE)
        tall = unpack(sums[chunk][0], crossed, chunk, width, list(tall))
    blocks = [tall[0]] + [send(tall[i], across(*OTHERS[i])) for i in range(1, 8)]

    def block_row(z_at, yh_at, half):
        return (z_at * 2 + yh_at) * (columns // width) + (c + half) % 2 * (columns // width // 2)

    rows_in = [block_row((z + 4 - dz) % 4, (yh + m) % 2, half) for m, dz in OTHERS for half in range(2)]
    rows_out = [block_row((z + dz) % 4, (yh + m) % 2, half) for m, dz in OTHERS for half in range(2)]
    orbit_grad, *leaving = taylor(jnp.stack(rows_in + rows_out).astype(jnp.int32), orbitals, cotangent, blocks)

    arrived = [leaving[0]] + [send(leaving[i], across(*OTHERS[i])) for i in range(1, 8)]
    arrived = [arrived[m * 4 + (4 - dz) % 4] for m, dz in OTHERS]
    gathered, after = [None] * CHUNKS, arrived[0]
    for chunk in PACKED:
        own, crossing = pack(arrived, chunk, after)
        after = own
        rows = jnp.concatenate([own, send(crossing, CORE)], axis=0)
        gathered[chunk] = gather_side_last(rows) if chunk == 0 else gather_side_first(rows)
    field = jnp.zeros((2 * vec_rows, walkers), F32)
    chol_grad = None
    leaving = []
    for turn, chunk in enumerate(FINISHED):
        given = (at, fields_rel, cholesky, others[chunk])
        if turn < 2:
            chol_grad, other, field = finish(*given, field, gathered[chunk], chunk, chol_grad)
        else:
            chol_grad = place(at, leaving[:1], FINISHED[:1], chol_grad)
            (field,) = finish(*given, field, gathered[chunk], chunk, None, do_chol=False)
            chol_grad, other = finish(*given, field, gathered[chunk], chunk, chol_grad, do_field=False)
        leaving.append(send(other, CORE))

    natural = lax.dot_general(
        field, order.astype(F32), (((1,), (1,)), ((), ())), precision=lax.Precision.HIGHEST, preferred_element_type=F32
    )
    summed = natural[:vec_rows] + send(natural[vec_rows:].astype(BF16), CORE).astype(F32)
    n_pair = lax.axis_size("pair")
    apart = summed.astype(BF16).reshape(vec_rows, n_pair, walkers // n_pair).transpose(1, 0, 2)
    field_grad = lax.all_to_all(apart, "pair", split_axis=0, concat_axis=0, tiled=True).astype(F32).sum(axis=0)
    chol_grad = place(at, leaving[1:], FINISHED[1:], chol_grad)
    return (orbit_grad, chol_grad, field_grad)


def solution(mesh):
    in_specs = (
        P("walk", "pair"),
        P(),
        P(("pair", "walk"), None, None),
        P(("pair", "walk"), None, None),
    )
    out_specs = (P(("pair", "walk"), None, None), P("walk", "pair"), P("walk", "pair"))

    return jax.shard_map(on_device, mesh=mesh, in_specs=in_specs, out_specs=out_specs, check_vma=False)
```

```python
import functools

import jax
import jax.numpy as jnp
from jax import lax
from jax.experimental import pallas as pl
from jax.experimental.pallas import tpu as pltpu
from jax.sharding import PartitionSpec as P


BF16 = jnp.bfloat16
F32 = jnp.float32
ALL = ("pair", "walk")
CHUNKS = 3
REDUCED = (1, 2, 0)
SUMMED = (1, 0, 2)
PACKED = (1, 0, 2)
FINISHED = (1, 0, 2)
BLOCK = 4096
PLACED = 4
LANES = 128
VMEM = pl.BlockSpec(memory_space=pltpu.VMEM)


def moved(to):
    pairs = []
    for z in range(4):
        for yh in range(2):
            for x in range(4):
                for yl in range(2):
                    for c in range(2):
                        z2, yh2, x2, yl2, c2 = to(z, yh, x, yl, c)
                        here = ((z * 2 + yh) * 4 + x) * 4 + yl * 2 + c
                        there = (((z2 % 4) * 2 + yh2 % 2) * 4 + x2 % 4) * 4 + (yl2 % 2) * 2 + c2 % 2
                        pairs.append((here, there))
    return pairs


CORE = moved(lambda z, yh, x, yl, c: (z, yh, x, yl, c + 1))
SIDE = moved(lambda z, yh, x, yl, c: (z, yh, x, yl + 1, c))
UP = moved(lambda z, yh, x, yl, c: (z, yh, x + 1, yl, c))
DOWN = moved(lambda z, yh, x, yl, c: (z, yh, x + 3, yl, c))
OTHERS = [(m, dz) for m in range(2) for dz in range(4)]


def across(m, dz):
    return moved(lambda z, yh, x, yl, c: (z + dz, yh + m, x, yl + m, c))


def send(array, pairs):
    return lax.ppermute(array, ALL, pairs)


def tied(array, *others):
    return lax.optimization_barrier((array, *others))[0]


def added(*terms):
    total = terms[0].astype(F32)
    for term in terms[1:]:
        total = total + term.astype(F32)
    return total.astype(BF16)


def whole(shape):
    return pl.BlockSpec(shape, lambda *_: (0,) * len(shape))


def take_kernel(start, step, at_ref, all_ref, out_ref, sems):
    column = pl.multiple_of((1 - at_ref[0]) * step + start, LANES)
    copies = []
    for n in range(out_ref.shape[0] // 16):
        rows = slice(16 * n, 16 * n + 16)
        copies.append(
            pltpu.make_async_copy(all_ref.at[rows, pl.ds(column, out_ref.shape[1])], out_ref.at[rows, :], sems.at[n])
        )
    for copy in copies:
        copy.start()
    for copy in copies:
        copy.wait()


def take(at, cholesky, chunk, chunk_width):
    rows = cholesky.shape[0]
    return pl.pallas_call(
        functools.partial(take_kernel, chunk * chunk_width, CHUNKS * chunk_width),
        grid_spec=pltpu.PrefetchScalarGridSpec(
            num_scalar_prefetch=1,
            grid=(1,),
            in_specs=[pl.BlockSpec(memory_space=pl.ANY)],
            out_specs=VMEM,
            scratch_shapes=[pltpu.SemaphoreType.DMA((rows // 16,))],
        ),
        out_shape=jax.ShapeDtypeStruct((rows, chunk_width), BF16),
        name="take",
    )(at, cholesky)


def partial_kernel(groups, at_ref, weights_ref, own_ref, other_ref, after_ref, *outs):
    here = pl.ds(pl.multiple_of(pl.program_id(0) * BLOCK, BLOCK), BLOCK)
    rows = jnp.concatenate([own_ref[...], other_ref[:, here]], axis=0)
    sums = jnp.dot(weights_ref[...], rows, preferred_element_type=F32).astype(BF16)
    for group, out in zip(groups, outs):
        for place, start in enumerate(group):
            out[place * 16 : place * 16 + 16, :] = sums[start : start + 16]


def partial_sums(at, weights, cholesky, other, chunk, groups, after):
    rows, width = other.shape
    steps = width // BLOCK
    return pl.pallas_call(
        functools.partial(partial_kernel, groups),
        grid_spec=pltpu.PrefetchScalarGridSpec(
            num_scalar_prefetch=1,
            grid=(steps,),
            in_specs=[
                whole(weights.shape),
                pl.BlockSpec((rows, BLOCK), lambda i, at: (0, at[0] * (CHUNKS * steps) + chunk * steps + i)),
                VMEM,
                pl.BlockSpec(memory_space=pl.ANY),
            ],
            out_specs=[pl.BlockSpec((16 * len(g), BLOCK), lambda i, at: (0, i)) for g in groups],
        ),
        out_shape=[jax.ShapeDtypeStruct((16 * len(g), width), BF16) for g in groups],
        cost_estimate=pl.CostEstimate(flops=2 * 128 * 128 * width, bytes_accessed=512 * width, transcendentals=0),
        name="partial_sums",
    )(at, weights, cholesky, other, after)


def unpack_kernel(depth, width, n_own, has_outs, *refs):
    own, other = refs[:n_own], refs[n_own : n_own + 1]
    outs, scratch = refs[n_own + 1 + 8 * has_outs : -1], refs[-1]
    across_lanes = width // LANES
    for half, parts in enumerate((own, other)):
        for tile in range(depth * across_lanes):
            lanes = slice(tile * LANES, (tile + 1) * LANES)
            total = parts[0][0:8, lanes].astype(F32)
            for part in parts[1:]:
                total = total + part[0:8, lanes].astype(F32)
            scratch[half, tile * 8 : tile * 8 + 8, :] = total
        for walker in range(8):
            for lane in range(across_lanes):
                tall = [
                    scratch[half, pl.ds((top * across_lanes + lane) * 8 + walker, 8, stride=8 * across_lanes), :]
                    for top in range(0, depth, 8)
                ]
                block = jnp.concatenate(tall, axis=0).astype(BF16)
                outs[walker][half, :, lane * LANES : (lane + 1) * LANES] = block


def unpack(own, other, chunk, width, outs):
    depth = other.shape[1] // width
    arrays = [*own, other]
    specs = [pl.BlockSpec((8, depth * width), lambda i: (0, 0)) for _ in own] + [VMEM]
    aliases = {}
    if outs:
        aliases = {len(arrays) + n: n for n in range(8)}
        arrays += outs
        specs += [pl.BlockSpec(memory_space=pl.ANY)] * 8
    return pl.pallas_call(
        functools.partial(unpack_kernel, depth, width, len(own), int(bool(outs))),
        grid=(1,),
        in_specs=specs,
        out_specs=[pl.BlockSpec((2, depth, width), lambda i: (0, chunk, 0)) for _ in OTHERS],
        out_shape=[jax.ShapeDtypeStruct((2, CHUNKS * depth, width), BF16) for _ in OTHERS],
        scratch_shapes=[pltpu.VMEM((2, depth * width // LANES * 8, LANES), F32)],
        input_output_aliases=aliases,
        name="unpack",
    )(*arrays)


def pack_kernel(depth, width, *refs):
    blocks, own, other, scratch = refs[:8], refs[8], refs[9], refs[10]
    across_lanes = width // LANES
    for half, out in enumerate((own, other)):
        for walker in range(8):
            for lane in range(across_lanes):
                tall = blocks[walker][half, :, lane * LANES : (lane + 1) * LANES].astype(F32)
                for top in range(0, depth, 8):
                    rows = pl.ds((top * across_lanes + lane) * 8 + walker, 8, stride=8 * across_lanes)
                    scratch[half, rows, :] = tall[top : top + 8]
        for tile in range(depth * across_lanes):
            out[:, tile * LANES : (tile + 1) * LANES] = scratch[half, tile * 8 : tile * 8 + 8, :].astype(BF16)


def pack(blocks, chunk, after):
    _, rows, width = blocks[0].shape
    depth = rows // CHUNKS
    return pl.pallas_call(
        lambda *refs: pack_kernel(depth, width, *refs[:8], *refs[9:]),
        grid=(1,),
        in_specs=[pl.BlockSpec((2, depth, width), lambda i: (0, chunk, 0)) for _ in blocks]
        + [pl.BlockSpec(memory_space=pl.ANY)],
        out_specs=[VMEM] * 2,
        out_shape=[jax.ShapeDtypeStruct((8, depth * width), BF16)] * 2,
        scratch_shapes=[pltpu.VMEM((2, depth * width // LANES * 8, LANES), F32)],
        name="pack",
    )(*blocks, after)


def taylor_kernel(n_blocks, depths, at_ref, orbit_ref, cotan_ref, *refs):
    blocks, orbit_out, outs = refs[:n_blocks], refs[n_blocks], refs[n_blocks + 1 : 2 * n_blocks + 1]
    matrix, grad, series, adjoint = refs[2 * n_blocks + 1 :]
    width = matrix.shape[0]
    tile = 256
    for n, block in enumerate(blocks):
        for half in range(2):
            row = pl.multiple_of(at_ref[2 * n + half], 16)
            matrix[pl.ds(row, depths[n]), :] = block[half]
    series[0] = orbit_ref[0]
    adjoint[4] = cotan_ref[0]

    def tiles(body):
        for start in range(0, width, tile):
            body(slice(start, start + tile))

    for degree in (1, 2, 3):
        down = 4 - degree

        def both(at, degree=degree, down=down):
            product = lax.dot_general(
                series[degree - 1], matrix[at, :], (((1,), (1,)), ((), ())), preferred_element_type=F32
            )
            series[degree, :, at] = (product / degree).astype(BF16)
            product = jnp.dot(adjoint[down + 1], matrix[:, at], preferred_element_type=F32)
            adjoint[down, :, at] = (cotan_ref[0, :, at].astype(F32) + product / (down + 1)).astype(BF16)

        tiles(both)

    def last(at):
        product = jnp.dot(adjoint[1], matrix[:, at], preferred_element_type=F32)
        orbit_out[0, :, at] = (cotan_ref[0, :, at].astype(F32) + product).astype(BF16)
        total = None
        for degree in range(1, 5):
            term = lax.dot_general(
                adjoint[degree, :, at], series[degree - 1], (((0,), (0,)), ((), ())), preferred_element_type=F32
            )
            total = term if total is None else total + term / degree
        grad[at, :] = total.astype(BF16)

    tiles(last)
    for n, out in enumerate(outs):
        for half in range(2):
            row = pl.multiple_of(at_ref[2 * n_blocks + 2 * n + half], 16)
            out[half] = grad[pl.ds(row, depths[n]), :]


def taylor(at, orbitals, cotangent, blocks):
    width = orbitals.shape[2]
    n = len(blocks)
    specs = [VMEM] * n
    return pl.pallas_call(
        functools.partial(taylor_kernel, n, [block.shape[1] for block in blocks]),
        grid_spec=pltpu.PrefetchScalarGridSpec(
            num_scalar_prefetch=1,
            grid=(1,),
            in_specs=[VMEM, VMEM] + specs,
            out_specs=[VMEM] + specs,
            scratch_shapes=[
                pltpu.VMEM((width, width), BF16),
                pltpu.VMEM((width, width), BF16),
                pltpu.VMEM((4, orbitals.shape[1], width), BF16),
                pltpu.VMEM((5, orbitals.shape[1], width), BF16),
            ],
        ),
        out_shape=[jax.ShapeDtypeStruct(orbitals.shape, BF16)]
        + [jax.ShapeDtypeStruct(block.shape, BF16) for block in blocks],
        name="taylor",
    )(at, orbitals, cotangent, *blocks)


def field_kernel(n_parts, own_ref, other_ref, field_ref, *refs):
    grads = jnp.concatenate([part[...] for part in refs[:n_parts]], axis=0)
    rows = jnp.concatenate([own_ref[...], other_ref[...]], axis=0)
    refs[-1][...] += lax.dot_general(rows, grads, (((1,), (1,)), ((), ())), preferred_element_type=F32)


def chol_kernel(n_parts, weights_ref, *refs):
    grads = jnp.concatenate([part[...] for part in refs[:n_parts]], axis=0)
    total = jnp.dot(weights_ref[...], grads, preferred_element_type=F32).astype(BF16)
    chol_out, other_out = refs[-2:]
    half = total.shape[0] // 2
    chol_out[...] = total[:half]
    other_out[...] = total[half:]


def finish_kernel(n_parts, has_out, do_field, do_chol, at_ref, *refs):
    refs = list(refs)
    weights = [refs.pop(0)] if do_chol else []
    columns = [refs.pop(0) for _ in range(3)] if do_field else []
    parts, refs = refs[:n_parts], refs[n_parts + has_out :]
    if do_field:

        @pl.when(pl.program_id(0) == 0)
        def _():
            refs[-1][...] = columns[2][...]

        field_kernel(n_parts, *columns, *parts, refs[-1])
    if do_chol:
        chol_kernel(n_parts, *weights, *parts, *refs[:2])


def finish(at, weights, cholesky, other, field, parts, chunk, out, do_field=True, do_chol=True):
    rows, width = other.shape
    steps = width // BLOCK
    here = pl.BlockSpec((rows, BLOCK), lambda i, at: (0, at[0] * (CHUNKS * steps) + chunk * steps + i))
    along = pl.BlockSpec((rows, BLOCK), lambda i, at: (0, i))
    args, in_specs, out_specs, out_shape, aliases = [at], [], [], [], {}
    if do_chol:
        args.append(weights)
        in_specs.append(whole(weights.shape))
        out_specs += [here, along]
        out_shape += [jax.ShapeDtypeStruct(cholesky.shape, BF16), jax.ShapeDtypeStruct((rows, width), BF16)]
    if do_field:
        args += [cholesky, other, field]
        in_specs += [here, along, whole(field.shape)]
        out_specs.append(whole(field.shape))
        out_shape.append(jax.ShapeDtypeStruct(field.shape, F32))
    for part in parts:
        array, row = part if isinstance(part, tuple) else (part, None)
        height = array.shape[0] if row is None else 16
        args.append(array)
        in_specs.append(pl.BlockSpec((height, BLOCK), lambda i, at, row=row or 0: (row, i)))
    if do_chol and out is not None:
        aliases = {len(args): 0}
        args.append(out)
        in_specs.append(pl.BlockSpec(memory_space=pl.ANY))
    return pl.pallas_call(
        functools.partial(finish_kernel, len(parts), len(aliases), do_field, do_chol),
        grid_spec=pltpu.PrefetchScalarGridSpec(
            num_scalar_prefetch=1, grid=(steps,), in_specs=in_specs, out_specs=out_specs
        ),
        out_shape=out_shape,
        input_output_aliases=aliases,
        cost_estimate=pl.CostEstimate(flops=4 * 128 * 128 * width, bytes_accessed=768 * width, transcendentals=0),
        name="finish",
    )(*args)


def place_kernel(starts, step, at_ref, *refs):
    pieces, out_ref, sems = refs[: len(starts)], refs[len(starts) + 1], refs[len(starts) + 2]
    copies = []
    for n, (piece, start) in enumerate(zip(pieces, starts)):
        column = pl.multiple_of((1 - at_ref[0]) * step + start, LANES)
        for m in range(PLACED):
            rows = slice(m * piece.shape[0] // PLACED, (m + 1) * piece.shape[0] // PLACED)
            copies.append(
                pltpu.make_async_copy(
                    piece.at[rows, :], out_ref.at[rows, pl.ds(column, piece.shape[1])], sems.at[n * PLACED + m]
                )
            )
    for copy in copies:
        copy.start()
    for copy in copies:
        copy.wait()


def place(at, pieces, chunks, out):
    width = pieces[0].shape[1]
    n = len(pieces)
    return pl.pallas_call(
        functools.partial(place_kernel, [chunk * width for chunk in chunks], CHUNKS * width),
        grid_spec=pltpu.PrefetchScalarGridSpec(
            num_scalar_prefetch=1,
            grid=(1,),
            in_specs=[VMEM] * n + [pl.BlockSpec(memory_space=pl.ANY)],
            out_specs=pl.BlockSpec(memory_space=pl.ANY),
            scratch_shapes=[pltpu.SemaphoreType.DMA((n * PLACED,))],
        ),
        out_shape=jax.ShapeDtypeStruct(out.shape, out.dtype),
        input_output_aliases={n + 1: 0},
        name="place",
    )(at, *pieces, out)


def reduce_side_last(parts, tie):
    far_up, far_down, near_up, free_up, free_down, near_down, here0, here1 = parts
    up, down = send(far_up, UP), send(far_down, DOWN)
    free_up, free_down = send(free_up, UP), send(free_down, DOWN)
    up, down = added(near_up, up), added(near_down, down)
    up, down = send(up, UP), send(down, DOWN)
    side = send(added(tied(here1, tie), free_up, down), SIDE)
    return [here0, up, free_down, side], [t[8:16] for t in (here0, up, free_down, side)]


def reduce_side_first(parts):
    leaving, staying = parts
    side = send(leaving, SIDE)

    def row(dx, half):
        rows = slice(dx * 16 + half * 8, dx * 16 + half * 8 + 8)
        return staying[rows], side[rows]

    far_up, far_down = lax.optimization_barrier((added(*row(2, 0)), added(*row(2, 1))))
    up, down = send(far_up, UP), send(far_down, DOWN)
    near_up = jnp.concatenate([added(*row(1, 0), up), added(*row(1, 1))], axis=0)
    near_down = jnp.concatenate([added(*row(3, 0)), added(*row(3, 1), down)], axis=0)
    up, down = send(near_up, UP), send(near_down, DOWN)
    return [staying, side, up, down], [t[8:16] for t in (staying, side, up, down)], (far_down, near_down)


def gather_side_first(rows):
    rows = jnp.concatenate([rows, send(rows, SIDE)], axis=0)
    low, high = send(rows, UP), send(rows, DOWN)
    far0, far1 = low[:16], high[16:]
    far0, far1 = send(far0, UP), send(far1, DOWN)
    return [rows, high, far0, far1, low]


def gather_side_last(rows):
    low, high = send(rows, UP), send(rows, DOWN)
    far0, far1 = send(low[:8], UP), send(high[8:], DOWN)
    rows_s = send(rows, SIDE)
    near_s = send(jnp.concatenate([high, low], axis=0), SIDE)
    far_s = send(jnp.concatenate([far0, far1], axis=0), SIDE)
    return [rows, rows_s, (high, 0), (near_s, 0), far0, far1, far_s, (low, 0), (near_s, 1)]


SIDE_LAST_GROUPS = ((64,), (80,), (32,), (48,), (96,), (112,), (0,), (16,))
SIDE_FIRST_GROUPS = ((16, 48, 80, 112), (0, 32, 64, 96))


def summed_of(at, weights, cholesky, others, chunk, after):
    groups = SIDE_FIRST_GROUPS if chunk == 0 else SIDE_LAST_GROUPS
    return partial_sums(at, weights, cholesky, others[chunk], chunk, groups, after)


def on_device(cholesky, fields, orbitals, cotangent):
    vec_rows, columns = cholesky.shape
    walkers = fields.shape[1]
    width = orbitals.shape[2]
    chunk_width = columns // (2 * CHUNKS)
    pair, walk = lax.axis_index("pair"), lax.axis_index("walk")
    z, yh = pair // 2, pair % 2
    x, yl, c = walk // 4, (walk // 2) % 2, walk % 2
    at = jnp.reshape(c, (1,)).astype(jnp.int32)

    r = lax.broadcasted_iota(jnp.int32, (walkers, walkers), 1)
    dx, dyl, dc, m, dz = r // 32, (r // 16) % 2, (r // 8) % 2, (r // 4) % 2, r % 4
    walker_z, walker_yh = (z + dz) % 4, (yh + m) % 2
    walker_x, walker_yl, walker_c = (x + dx) % 4, (yl + dyl + m) % 2, (c + dc) % 2
    walker = (walker_z * 2 + walker_yh) * 16 + walker_x * 4 + walker_yl * 2 + walker_c
    order = lax.broadcasted_iota(jnp.int32, (walkers, walkers), 0) == walker
    fields_here = jnp.concatenate(
        [
            lax.dynamic_slice_in_dim(fields, walk * vec_rows, vec_rows, 0),
            lax.dynamic_slice_in_dim(fields, (walk + 1 - 2 * c) * vec_rows, vec_rows, 0),
        ],
        axis=0,
    )
    fields_rel = jnp.dot(fields_here, order.astype(BF16), preferred_element_type=F32).astype(BF16)
    fields_turned = lax.dot_general(
        order.astype(BF16), fields_here, (((0,), (1,)), ((), ())), preferred_element_type=F32
    ).astype(BF16)

    others, sums, after, ties = [None] * CHUNKS, [None] * CHUNKS, fields_turned, None
    partials = [None] * CHUNKS
    for place_at, chunk in enumerate(SUMMED):
        whole_rows = cholesky if place_at < 2 else tied(cholesky, partials[SUMMED[0]][0])
        leaving = take(at, whole_rows, chunk, chunk_width)
        others[chunk] = send(leaving, CORE)
        if place_at == 1:
            partials[SUMMED[0]] = summed_of(at, fields_turned, cholesky, others, SUMMED[0], fields_turned)
    for last, chunk in zip(SUMMED, SUMMED[1:]):
        partials[chunk] = summed_of(at, fields_turned, cholesky, others, chunk, partials[last][0])
    *sums[0], ties = reduce_side_first(partials[0])
    for chunk in (1, 2):
        sums[chunk] = reduce_side_last(partials[chunk], ties[chunk - 1])
    tall = []
    for chunk in REDUCED:
        crossed = send(added(*sums[chunk][1]), CORE)
        tall = unpack(sums[chunk][0], crossed, chunk, width, list(tall))
    blocks = [tall[0]] + [send(tall[i], across(*OTHERS[i])) for i in range(1, 8)]

    def block_row(z_at, yh_at, half):
        return (z_at * 2 + yh_at) * (columns // width) + (c + half) % 2 * (columns // width // 2)

    rows_in = [block_row((z + 4 - dz) % 4, (yh + m) % 2, half) for m, dz in OTHERS for half in range(2)]
    rows_out = [block_row((z + dz) % 4, (yh + m) % 2, half) for m, dz in OTHERS for half in range(2)]
    orbit_grad, *leaving = taylor(jnp.stack(rows_in + rows_out).astype(jnp.int32), orbitals, cotangent, blocks)

    arrived = [leaving[0]] + [send(leaving[i], across(*OTHERS[i])) for i in range(1, 8)]
    arrived = [arrived[m * 4 + (4 - dz) % 4] for m, dz in OTHERS]
    gathered, after = [None] * CHUNKS, arrived[0]
    for chunk in PACKED:
        own, crossing = pack(arrived, chunk, after)
        after = own
        rows = jnp.concatenate([own, send(crossing, CORE)], axis=0)
        gathered[chunk] = gather_side_last(rows) if chunk == 0 else gather_side_first(rows)
    field = jnp.zeros((2 * vec_rows, walkers), F32)
    chol_grad = None
    leaving = []
    for chunk in FINISHED:
        given = (at, fields_rel, cholesky, others[chunk])
        if chunk == FINISHED[-1]:
            chol_grad = place(at, leaving, FINISHED[:-1], chol_grad)
            leaving = []
        if chunk != FINISHED[-1]:
            chol_grad, other, field = finish(*given, field, gathered[chunk], chunk, chol_grad)
        else:
            (field,) = finish(*given, field, gathered[chunk], chunk, None, do_chol=False)
            chol_grad, other = finish(*given, field, gathered[chunk], chunk, chol_grad, do_field=False)
        leaving.append(send(other, CORE))

    natural = lax.dot_general(
        field, order.astype(F32), (((1,), (1,)), ((), ())), precision=lax.Precision.HIGHEST, preferred_element_type=F32
    )
    summed = natural[:vec_rows] + send(natural[vec_rows:].astype(BF16), CORE).astype(F32)
    n_pair = lax.axis_size("pair")
    apart = summed.astype(BF16).reshape(vec_rows, n_pair, walkers // n_pair).transpose(1, 0, 2)
    field_grad = lax.all_to_all(apart, "pair", split_axis=0, concat_axis=0, tiled=True).astype(F32).sum(axis=0)
    chol_grad = place(at, leaving, FINISHED[-1:], chol_grad)
    return (orbit_grad, chol_grad, field_grad)


def solution(mesh):
    in_specs = (
        P("walk", "pair"),
        P(),
        P(("pair", "walk"), None, None),
        P(("pair", "walk"), None, None),
    )
    out_specs = (P(("pair", "walk"), None, None), P("walk", "pair"), P("walk", "pair"))

    return jax.shard_map(on_device, mesh=mesh, in_specs=in_specs, out_specs=out_specs, check_vma=False)
```
